256 devices in a mesh: dp: 4 (over x), space: 64 (over z, y, core).
Axes of the slice: x: 4, y: 4, z: 8, core: 2. Of those that a mesh axis runs over, the one named last changes fastest.
Arguments:
- fields: bfloat16 [4, 32, 6144, 128], P('dp', None, 'space'), may hold values from -6 to 6
- land_mask: int32 [6144, 128], P('space'), may hold values from 0 to 1, as said below
- land_frac: float32 [6144, 128], P('space'), may hold values from 0.05 to 1
- owner_map: int32 [12288], replicated, may hold values from 0 to 12287, as said below
- targets: float32 [4, 14, 12288], P('dp', None, 'space'), may hold values from -3 to 3
- conv_weight: bfloat16 [3, 3, 32, 128], replicated, may hold values from -0.375 to 0.375
- conv_bias: float32 [128], replicated, may hold values from -3 to 3
- mix_weight: bfloat16 [128, 128], replicated, may hold values from -0.5 to 0.5
- mix_bias: float32 [128], replicated, may hold values from -3 to 3
- out_weight: bfloat16 [128, 14], replicated, may hold values from -0.5 to 0.5
- out_bias: float32 [14], replicated, may hold values from -3 to 3
Outputs:
- coarse_pred: float32 [4, 14, 12288], P('dp', None, 'space')
- conv_grad: float32 [3, 3, 32, 128], replicated
- conv_bias_grad: float32 [128], replicated
- mix_grad: float32 [128, 128], replicated
- mix_bias_grad: float32 [128], replicated
- out_grad: float32 [128, 14], replicated
- out_bias_grad: float32 [14], replicated
- loss: float32 [], replicated
The draws below stay inside these ranges and needn't reach their ends.
Inputs may be any that keep to these rules, and one draw needn't show every extreme that they name: A permutation. Coarse cell g is owned by index owner_map[g] // 192 of space, at local place owner_map[g] % 192; the 192 coarse cells of every strip go to every owner exactly 3 at a time. `land_mask`: 1 marks land.
All inputs are finite; a program needn't handle non-finite values.
Results may differ from the reference program's by a relative error of at most 0.00039.
Values may be sent and summed in bfloat16 or wider, within the bound.
A program may use at most 128 MiB of HBM per device.

```python
import math
import jax
import jax.numpy as jnp
from jax import lax

WIDTH = 128
POOLS = 14
CHANNELS = 32
SIDE = 8
ROWS = 96
COLUMNS = 128
MEMBERS = 4
ALL_ROWS = 6144
BLOCKS = 192
COARSE = 12288
CAPACITY = 3
N_SPACE = 64


def draw_owner_map(key, part):
    strip_keys = jax.random.split(jax.random.fold_in(key, 11), N_SPACE)
    shuffled = jax.vmap(lambda single: jax.random.permutation(single, BLOCKS))(strip_keys)
    owners = (shuffled // CAPACITY).reshape(-1).astype(jnp.int32)
    breakers = jax.random.permutation(jax.random.fold_in(key, 12), COARSE).astype(jnp.int32)
    places = jnp.argsort(owners * COARSE + breakers)
    return jnp.zeros((COARSE,), jnp.int32).at[places].set(jnp.arange(COARSE, dtype=jnp.int32))


def draw_land_mask(key, part):
    share = jax.random.randint(jax.random.fold_in(key, 21), (ALL_ROWS // SIDE, COLUMNS // SIDE), 0, SIDE * SIDE + 1)
    picks = jax.random.randint(jax.random.fold_in(key, 22), (ALL_ROWS, COLUMNS), 0, SIDE * SIDE)
    share_cells = jnp.repeat(jnp.repeat(share, SIDE, axis=0), SIDE, axis=1)
    return (picks < share_cells).astype(jnp.int32)


def shard_levels(rng, shape, cuts, low, top_value):
    factor_of = 1.0
    for position, blocks in cuts:
        draws = jax.random.uniform(jax.random.fold_in(jax.random.fold_in(rng, 6), position), (blocks,), jnp.float32, low / len(cuts), top_value / len(cuts))
        factor_of = factor_of * jnp.repeat(jnp.exp(draws), shape[position] // blocks).reshape((-1,) + (1,) * (len(shape) - 1 - position))
    return factor_of


def normal_values(rng, extent, deviation, most, cuts=(), kind=jnp.bfloat16):
    array = jax.random.normal(rng, extent, jnp.float32) * deviation
    if len(cuts) > 0:
        array = shard_levels(rng, extent, cuts, -0.22, 0.18) * array
    return jnp.clip(array, min=-most, max=most).astype(kind)


def setup_inputs(seed: int = 0) -> dict:
    splits = jax.random.split(jax.random.key(seed), 12)
    fields = normal_values(splits[0], (MEMBERS, CHANNELS, ALL_ROWS, COLUMNS), 1.0, 6.0, ((0, 4), (2, 64)))
    land_mask = draw_land_mask(jax.random.fold_in(splits[11], 71), 0)
    land_frac = jnp.clip(0.05 + 0.95 * jax.random.uniform(splits[2], (ALL_ROWS, COLUMNS), jnp.float32) ** shard_levels(splits[2], (ALL_ROWS, COLUMNS), ((0, 64),), -0.2, 0.2), 0.05, 1.0)
    owner_map = draw_owner_map(jax.random.fold_in(splits[11], 71), 0)
    targets = normal_values(splits[4], (MEMBERS, POOLS, COARSE), 0.5, 3.0, ((0, 4), (2, 64)), jnp.float32)
    conv_weight = normal_values(splits[5], (3, 3, CHANNELS, WIDTH), (9 * CHANNELS) ** -0.5, 0.375)
    conv_bias = normal_values(splits[6], (WIDTH,), 0.5, 3.0, (), jnp.float32)
    mix_weight = normal_values(splits[7], (WIDTH, WIDTH), WIDTH ** -0.5, 0.5)
    mix_bias = normal_values(splits[8], (WIDTH,), 0.5, 3.0, (), jnp.float32)
    out_weight = normal_values(splits[9], (WIDTH, POOLS), WIDTH ** -0.5, 0.5)
    out_bias = normal_values(splits[10], (POOLS,), 0.5, 3.0, (), jnp.float32)
    return dict(fields=fields, land_mask=land_mask, land_frac=land_frac, owner_map=owner_map, targets=targets, conv_weight=conv_weight, conv_bias=conv_bias, mix_weight=mix_weight, mix_bias=mix_bias, out_weight=out_weight, out_bias=out_bias)


CUBIC = 0.044715
ROOT_TWO_PI = math.sqrt(2.0 / math.pi)

def gelu_pair(pre):
    inner = ROOT_TWO_PI * (pre + CUBIC * pre * pre * pre)
    tanh_value = jnp.tanh(inner)
    value = 0.5 * pre * (1.0 + tanh_value)
    slope = 0.5 * (1.0 + tanh_value) + 0.5 * pre * (1.0 - tanh_value * tanh_value) * ROOT_TWO_PI * (1.0 + 3.0 * CUBIC * pre * pre)
    return (value, slope)

def product(form, left, right):
    return jnp.einsum(form, left.astype(jnp.float32), right.astype(jnp.float32))

def block_sums(values, side):
    leading = values.shape[:-2]
    height, breadth = (values.shape[-2], values.shape[-1])
    shaped = values.reshape(leading + (height // side, side, breadth // side, side))
    return lax.optimization_barrier(jnp.sum(shaped, axis=(-3, -1))).reshape(leading + (height // side * (breadth // side),))

def forward_tile(padded, conv_weight, conv_bias, mix_weight, mix_bias, out_weight, out_bias):
    height = padded.shape[2] - 2
    breadth = padded.shape[3] - 2
    pieces = [padded[:, :, row_shift:row_shift + height, col_shift:col_shift + breadth] for row_shift in range(3) for col_shift in range(3)]
    stacked = jnp.concatenate(pieces, axis=1)
    flat_weight = conv_weight.reshape(-1, conv_weight.shape[3])
    pre_one = product('mkrc,kh->mrch', stacked, flat_weight) + conv_bias
    value_one, slope_one = gelu_pair(pre_one)
    hidden_one = value_one.astype(jnp.bfloat16)
    pre_two = product('mrch,hg->mrcg', hidden_one, mix_weight) + mix_bias
    value_two, slope_two = gelu_pair(pre_two)
    hidden_two = value_two.astype(jnp.bfloat16)
    raw = product('mrch,hp->mprc', hidden_two, out_weight) + out_bias[None, :, None, None]
    return (stacked, slope_one, hidden_one, slope_two, hidden_two, raw)

def backward_tile(stacked, slope_one, hidden_one, slope_two, hidden_two, raw, weight_map, d_block, mix_weight, out_weight, side):
    members, pools = (d_block.shape[0], d_block.shape[1])
    height, breadth = weight_map.shape
    d_cells = d_block.reshape(members, pools, height // side, breadth // side)
    d_cells = jnp.repeat(jnp.repeat(d_cells, side, axis=2), side, axis=3)
    d_raw = (d_cells * weight_map * jax.nn.sigmoid(raw)).astype(jnp.bfloat16)
    out_grad = product('mrch,mprc->hp', hidden_two, d_raw)
    out_bias_grad = lax.optimization_barrier(jnp.sum(d_raw.astype(jnp.float32), axis=(0, 2, 3)))
    d_two = (product('mprc,hp->mrch', d_raw, out_weight) * slope_two).astype(jnp.bfloat16)
    mix_grad = product('mrch,mrcg->hg', hidden_one, d_two)
    mix_bias_grad = lax.optimization_barrier(jnp.sum(d_two.astype(jnp.float32), axis=(0, 1, 2)))
    d_one = (product('mrcg,hg->mrch', d_two, mix_weight) * slope_one).astype(jnp.bfloat16)
    conv_grad = product('mkrc,mrch->kh', stacked, d_one)
    conv_bias_grad = lax.optimization_barrier(jnp.sum(d_one.astype(jnp.float32), axis=(0, 1, 2)))
    return (conv_grad, conv_bias_grad, mix_grad, mix_bias_grad, out_grad, out_bias_grad)

def reference(fields, land_mask, land_frac, owner_map, targets, conv_weight, conv_bias, mix_weight, mix_bias, out_weight, out_bias):
    padded_all = jnp.pad(fields, ((0, 0), (0, 0), (1, 1), (1, 1)))
    weight_all = land_frac * land_mask.astype(jnp.float32)
    tiles = MEMBERS * N_SPACE
    zero = jnp.zeros((), jnp.int32)

    def tile_inputs(serial):
        member = (serial // N_SPACE).astype(jnp.int32)
        strip = (serial % N_SPACE).astype(jnp.int32)
        slab = lax.dynamic_slice(padded_all, (member, zero, strip * ROWS, zero), (1, CHANNELS, ROWS + 2, COLUMNS + 2))
        weight_map = lax.dynamic_slice(weight_all, (strip * ROWS, zero), (ROWS, COLUMNS))
        return (member, strip, slab, weight_map)

    def first_pass(serial):
        member, strip, slab, weight_map = tile_inputs(serial)
        outputs = forward_tile(slab, conv_weight, conv_bias, mix_weight, mix_bias, out_weight, out_bias)
        density = jax.nn.softplus(outputs[5]) * weight_map
        return block_sums(density, SIDE)[0]
    serials = jnp.arange(tiles, dtype=jnp.int32)
    sums = lax.map(first_pass, serials)
    sums = sums.reshape(MEMBERS, N_SPACE, POOLS, BLOCKS).transpose(0, 2, 1, 3).reshape(MEMBERS, POOLS, COARSE)
    denom_global = jnp.maximum(block_sums(weight_all, SIDE), 1.0)
    coarse_global = sums / denom_global
    coarse_pred = jnp.zeros((MEMBERS, POOLS, COARSE), jnp.float32).at[:, :, owner_map].set(coarse_global)
    residual_global = coarse_global - targets[:, :, owner_map]
    count_all = MEMBERS * POOLS * COARSE
    loss = 0.5 * jnp.sum(residual_global * residual_global) / count_all
    d_global = residual_global / (math.sqrt(count_all) * denom_global)

    def second_pass(carry, serial):
        member, strip, slab, weight_map = tile_inputs(serial)
        outputs = forward_tile(slab, conv_weight, conv_bias, mix_weight, mix_bias, out_weight, out_bias)
        d_block = lax.dynamic_slice(d_global, (member, zero, strip * BLOCKS), (1, POOLS, BLOCKS))
        grads = backward_tile(*outputs, weight_map, d_block, mix_weight, out_weight, SIDE)
        return (tuple((first + second for first, second in zip(carry, grads))), None)
    initial = (jnp.zeros((9 * CHANNELS, WIDTH), jnp.float32), jnp.zeros((WIDTH,), jnp.float32), jnp.zeros((WIDTH, WIDTH), jnp.float32), jnp.zeros((WIDTH,), jnp.float32), jnp.zeros((WIDTH, POOLS), jnp.float32), jnp.zeros((POOLS,), jnp.float32))
    grads, _ = lax.scan(second_pass, initial, serials)
    conv_grad = grads[0].reshape(3, 3, CHANNELS, WIDTH)
    return (coarse_pred, conv_grad, grads[1], grads[2], grads[3], grads[4], grads[5], loss)
```

```python
import functools
import math

import jax
import jax.numpy as jnp
from jax import lax
from jax.experimental import pallas as pl
from jax.experimental.pallas import tpu as pltpu
from jax.sharding import PartitionSpec as P

SIDE = 8


CUBIC = 0.044715
ROOT_TWO_PI = math.sqrt(2.0 / math.pi)


def halo_rows(block):
    count = lax.axis_size("space")
    forward = [(i, i + 1) for i in range(count - 1)]
    backward = [(target, source) for source, target in forward]
    above = lax.ppermute(block[-1:], "space", forward)
    below = lax.ppermute(block[:1], "space", backward)
    return above, below


def gelu_pair(pre):
    inner = ROOT_TWO_PI * (pre + CUBIC * pre * pre * pre)
    tanh_value = jnp.tanh(inner)
    value = 0.5 * pre * (1.0 + tanh_value)
    slope = 0.5 * (1.0 + tanh_value) + 0.5 * pre * (1.0 - tanh_value * tanh_value) * ROOT_TWO_PI * (
        1.0 + 3.0 * CUBIC * pre * pre
    )
    return (value, slope)


MESH = pl.DeviceIdType.MESH
EXACT = lax.Precision.HIGHEST
TURNS = 16
LINES = 32
PART = 2
SLOTS = 3
LANES = 16


def pack(values, picks):
    peers = picks[0].shape[0]
    rows = [
        lax.dot_general(values, pick, (((1,), (1,)), ((), ())), precision=EXACT, preferred_element_type=jnp.float32)
        for pick in picks
    ]
    rows.append(jnp.zeros((128 - LANES * len(picks), peers), jnp.float32))
    return jnp.concatenate(rows, axis=0).T


def unpack(block, picks):
    turned = block.T
    total = None
    for slot, pick in enumerate(picks):
        term = jnp.dot(
            turned[LANES * slot : LANES * (slot + 1)], pick, precision=EXACT, preferred_element_type=jnp.float32
        )
        total = term if total is None else total + term
    return total


def owner_picks(owners, me, blocks):
    peers = owners.shape[0]
    local = owners - me * blocks
    match = ((local >= 0) & (local < blocks)).astype(jnp.float32)
    row = lax.broadcasted_iota(jnp.int32, (blocks, blocks), 0)
    col = lax.broadcasted_iota(jnp.int32, (blocks, blocks), 1)
    before = (row < col).astype(jnp.float32)
    earlier = jnp.dot(match.astype(jnp.bfloat16), before.astype(jnp.bfloat16), preferred_element_type=jnp.float32)
    place = lax.broadcasted_iota(jnp.int32, (peers, blocks), 1).astype(jnp.float32)
    picks = []
    for slot in range(SLOTS):
        mine = match * (earlier == float(slot)).astype(jnp.float32)
        spot = jnp.sum(mine * local.astype(jnp.float32), axis=1, keepdims=True)
        picks.append((place == spot).astype(jnp.float32))
    return picks


def strip_picks(owned, peers, blocks):
    scaled = (owned.astype(jnp.float32) + 0.5) * (1.0 / blocks)
    target = jnp.floor(scaled)
    row = lax.broadcasted_iota(jnp.int32, (blocks, blocks), 0)
    col = lax.broadcasted_iota(jnp.int32, (blocks, blocks), 1)
    spread = jnp.broadcast_to(target, (blocks, blocks))
    column = jnp.sum(jnp.where(row == col, spread, 0.0), axis=1, keepdims=True)
    same = jnp.where((column == spread) & (row < col), 1.0, 0.0)
    rank = jnp.sum(same, axis=0, keepdims=True)
    peer = lax.broadcasted_iota(jnp.int32, (peers, blocks), 0).astype(jnp.float32)
    return [
        ((peer == target) & (rank == float(slot))).astype(jnp.float32) for slot in range(SLOTS)
    ]


def row_copy(peers, me, step, send_ref, recv_ref, send_sems, recv_sems):
    peer = lax.rem(me + step, peers)
    return pltpu.make_async_remote_copy(
        src_ref=send_ref.at[peer],
        dst_ref=recv_ref.at[me],
        send_sem=send_sems.at[step],
        recv_sem=recv_sems.at[step],
        device_id=(lax.axis_index("dp"), peer),
        device_id_type=MESH,
    )


def targets_kernel(
    peers, blocks, owners_ref, targets_ref, strip_ref, owner_ref, here_ref,
    send, recv, held, send_sems, recv_sems
):
    me = lax.axis_index("space")
    dp = lax.axis_index("dp")
    barrier = pltpu.get_barrier_semaphore()

    def greet(step, carry):
        pl.semaphore_signal(
            barrier, inc=1, device_id=(dp, lax.rem(me + step, peers)), device_id_type=MESH
        )
        return carry

    lax.fori_loop(1, peers, greet, 0)
    picks = owner_picks(owners_ref[...], me, blocks)
    for slot in range(SLOTS):
        owner_ref[slot] = picks[slot]
    pools = targets_ref.shape[0]
    held[...] = jnp.zeros_like(held)
    held[0:pools, :] = targets_ref[...]
    send[:, 0, :] = pack(held[...], picks)
    strip = strip_picks(owners_ref[pl.ds(me, 1), :], peers, blocks)
    for slot in range(SLOTS):
        strip_ref[slot] = strip[slot]
    pl.semaphore_wait(barrier, peers - 1)

    def begin(step, carry):
        row_copy(peers, me, step, send, recv, send_sems, recv_sems).start()
        return carry

    def finish(step, carry):
        row_copy(peers, me, step, send, recv, send_sems, recv_sems).wait()
        return carry

    lax.fori_loop(1, peers, begin, 0)
    recv[pl.ds(me, 1)] = send[pl.ds(me, 1)]
    lax.fori_loop(1, peers, finish, 0)
    here_ref[...] = unpack(recv[:, 0, :], strip)


def reduce_kernel(
    peers, ways, grads_ref, pred_ref, strip_ref, owner_ref, out_ref, coarse_ref,
    send, recv, got, part, got_part, whole, send_sems, recv_sems, out_sems, in_sems, own_sem
):
    me = lax.axis_index("space")
    x = lax.axis_index("dp")
    span = ways * 2
    z = me // span
    y = lax.rem(me, span) // 2
    core = lax.rem(me, 2)
    flat = x * ways + y
    deep = z * 2 + core

    def plane(step):
        other = lax.rem(flat + step, TURNS)
        return other, (other // ways, z * span + lax.rem(other, ways) * 2 + core)

    def line(step):
        other = lax.rem(deep + step, TURNS)
        return other, (x, (other // 2) * span + y * 2 + lax.rem(other, 2))

    barrier = pltpu.get_barrier_semaphore()

    def greet(step, carry):
        pl.semaphore_signal(barrier, inc=1, device_id=(x, lax.rem(me + step, peers)), device_id_type=MESH)
        return carry

    def greet_plane(step, carry):
        pl.semaphore_signal(barrier, inc=1, device_id=plane(step)[1], device_id_type=MESH)
        return carry

    lax.fori_loop(1, peers, greet, 0)
    lax.fori_loop(1, TURNS, greet_plane, 0)
    send[:, 0, :] = pack(pred_ref[...], [strip_ref[slot] for slot in range(SLOTS)])
    pl.semaphore_wait(barrier, peers - 1 + TURNS - 1)

    def remote(src, dst, phase, step, device):
        return pltpu.make_async_remote_copy(
            src_ref=src,
            dst_ref=dst,
            send_sem=out_sems.at[phase, step],
            recv_sem=in_sems.at[phase, step],
            device_id=device,
            device_id_type=MESH,
        )

    def scatter_plane(step):
        other, device = plane(step)
        return remote(grads_ref.at[other], got.at[step - 1], 0, step, device)

    def scatter_line(step):
        other, device = line(step)
        return remote(part.at[other], got_part.at[step - 1], 1, step, device)

    def gather_line(step):
        return remote(whole.at[deep], whole.at[deep], 2, step, line(step)[1])

    def gather_plane(step):
        return remote(out_ref.at[flat], out_ref.at[flat], 3, step, plane(step)[1])

    def start_all(build):
        def body(step, carry):
            build(step).start()
            return carry

        lax.fori_loop(1, TURNS, body, 0)

    def wait_all(build):
        def body(step, carry):
            build(step).wait()
            return carry

        lax.fori_loop(1, TURNS, body, 0)

    start_all(scatter_plane)

    def begin(step, carry):
        row_copy(peers, me, step, send, recv, send_sems, recv_sems).start()
        return carry

    def finish(step, carry):
        row_copy(peers, me, step, send, recv, send_sems, recv_sems).wait()
        return carry

    lax.fori_loop(1, peers, begin, 0)
    recv[pl.ds(me, 1)] = send[pl.ds(me, 1)]

    wait_all(scatter_plane)
    total = grads_ref[flat]
    for step in range(TURNS - 1):
        total = total + got[step]
    for turn in range(TURNS):
        part[turn] = total[PART * turn : PART * (turn + 1)]
    start_all(scatter_line)
    wait_all(scatter_line)
    piece = part[deep]
    for step in range(TURNS - 1):
        piece = piece + got_part[step]
    whole[deep] = piece
    start_all(gather_line)
    wait_all(gather_line)
    own = pltpu.make_async_copy(whole, out_ref.at[flat], own_sem)
    own.start()
    own.wait()
    start_all(gather_plane)
    lax.fori_loop(1, peers, finish, 0)
    coarse_ref[...] = unpack(recv[:, 0, :], [owner_ref[slot] for slot in range(SLOTS)])
    wait_all(gather_plane)


def vmem(count):
    return [pl.BlockSpec(memory_space=pltpu.VMEM)] * count


def route_targets(owner_map, targets, peers, blocks):
    picks = jax.ShapeDtypeStruct((SLOTS, peers, blocks), jnp.float32)
    return pl.pallas_call(
        functools.partial(targets_kernel, peers, blocks),
        out_shape=(picks, picks, jax.ShapeDtypeStruct((LANES, blocks), jnp.float32)),
        in_specs=vmem(2),
        out_specs=tuple(vmem(3)),
        scratch_shapes=[
            pltpu.VMEM((peers, 1, 128), jnp.float32),
            pltpu.VMEM((peers, 1, 128), jnp.float32),
            pltpu.VMEM((LANES, blocks), jnp.float32),
            pltpu.SemaphoreType.DMA((peers,)),
            pltpu.SemaphoreType.DMA((peers,)),
        ],
        compiler_params=pltpu.CompilerParams(collective_id=0, has_side_effects=True),
        name="route_targets",
    )(owner_map.reshape(peers, blocks), targets)


def reduce_all(grads, pred, strip, owner, peers, blocks):
    ways = lax.axis_size("dp")
    return pl.pallas_call(
        functools.partial(reduce_kernel, peers, ways),
        out_shape=(
            jax.ShapeDtypeStruct((TURNS, TURNS, PART, 128), jnp.float32),
            jax.ShapeDtypeStruct((LANES, blocks), jnp.float32),
        ),
        in_specs=vmem(4),
        out_specs=tuple(vmem(2)),
        scratch_shapes=[
            pltpu.VMEM((peers, 1, 128), jnp.float32),
            pltpu.VMEM((peers, 1, 128), jnp.float32),
            pltpu.VMEM((TURNS - 1, LINES, 128), jnp.float32),
            pltpu.VMEM((TURNS, PART, 128), jnp.float32),
            pltpu.VMEM((TURNS - 1, PART, 128), jnp.float32),
            pltpu.VMEM((TURNS, PART, 128), jnp.float32),
            pltpu.SemaphoreType.DMA((peers,)),
            pltpu.SemaphoreType.DMA((peers,)),
            pltpu.SemaphoreType.DMA((4, TURNS)),
            pltpu.SemaphoreType.DMA((4, TURNS)),
            pltpu.SemaphoreType.DMA,
        ],
        compiler_params=pltpu.CompilerParams(collective_id=1, has_side_effects=True),
        name="reduce_all",
    )(grads, pred, strip, owner)


NT = (((1,), (1,)), ((), ()))
ONES = 16


def dot(left, right, dims=(((1,), (0,)), ((), ()))):
    return lax.dot_general(left, right, dims, preferred_element_type=jnp.float32)


def exact_dot(left, right, dims=(((1,), (0,)), ((), ()))):
    return lax.dot_general(left, right, dims, precision=EXACT, preferred_element_type=jnp.float32)


def column_of(row):
    width = row.shape[1]
    return jnp.broadcast_to(row, (width, width)).T[:, 0:1]


def shift_rows(block):
    wide = block.astype(jnp.float32)
    columns = wide.shape[2]
    place = lax.broadcasted_iota(jnp.int32, wide.shape, 2)
    left = jnp.where(place == 0, 0.0, pltpu.roll(wide, 1, 2))
    right = jnp.where(place == columns - 1, 0.0, pltpu.roll(wide, columns - 1, 2))
    return jnp.concatenate([left.astype(jnp.bfloat16), block, right.astype(jnp.bfloat16)], axis=1)


def network_kernel(
    count_all, pools, x_ref, above_ref, below_ref, frac_ref, mask_ref, here_ref,
    conv_ref, conv_bias_ref, mix_ref, mix_bias_ref, out_ref, out_bias_ref,
    flat_ref, pred_ref,
    shifted, stacked, row_buf, conv_acc, mix_acc, out_acc, bias_acc, square_acc
):
    rows, channels, columns = x_ref.shape
    taps, width = conv_ref.shape
    cells = SIDE * columns
    blocks = here_ref.shape[1]
    across = columns // SIDE

    shifted[0:1] = shift_rows(above_ref[...])
    shifted[rows + 1 : rows + 2] = shift_rows(below_ref[...])

    def shift_some(step, carry):
        shifted[pl.ds(step * SIDE + 1, SIDE)] = shift_rows(x_ref[pl.ds(step * SIDE, SIDE)])
        return carry

    lax.fori_loop(0, rows // SIDE, shift_some, 0)
    stacked[taps : taps + ONES, :] = jnp.ones((ONES, cells), jnp.bfloat16)

    conv_t = conv_ref[...].astype(jnp.float32).T.astype(jnp.bfloat16)
    mix = mix_ref[...]
    mix_t = mix.astype(jnp.float32).T.astype(jnp.bfloat16)
    row_buf[...] = jnp.zeros_like(row_buf)
    row_buf[0:pools, :] = out_ref[...].astype(jnp.float32)
    out_wide = row_buf[...]
    out_t = out_wide[0:LANES].astype(jnp.bfloat16)
    out_w = out_wide.T[:, 0:LANES].astype(jnp.bfloat16)
    row_buf[...] = jnp.zeros_like(row_buf)
    row_buf[0:1, 0:pools] = out_bias_ref[...]
    conv_bias = column_of(conv_bias_ref[...])
    mix_bias = column_of(mix_bias_ref[...])
    out_bias = column_of(row_buf[0:1, :])[0:LANES]

    conv_acc[...] = jnp.zeros_like(conv_acc)
    mix_acc[...] = jnp.zeros_like(mix_acc)
    out_acc[...] = jnp.zeros_like(out_acc)
    bias_acc[...] = jnp.zeros_like(bias_acc)
    square_acc[...] = jnp.zeros_like(square_acc)
    pred_ref[...] = jnp.zeros_like(pred_ref)
    here = here_ref[...]
    scale = math.sqrt(count_all)

    def tile(step, carry):
        base = step * SIDE
        for line in range(SIDE):
            window = shifted[pl.ds(base + line, 3)]
            stacked[0:taps, line * columns : (line + 1) * columns] = window.reshape(taps, columns)
        patch = stacked[0:taps, :]
        pre_one = dot(conv_t, patch) + conv_bias
        value_one, slope_one = gelu_pair(pre_one)
        hidden_one = value_one.astype(jnp.bfloat16)
        pre_two = dot(mix_t, hidden_one) + mix_bias
        value_two, slope_two = gelu_pair(pre_two)
        hidden_two = value_two.astype(jnp.bfloat16)
        raw = dot(out_t, hidden_two) + out_bias
        window = pl.ds(pl.multiple_of(base, SIDE), SIDE)
        weight = frac_ref[window, :] * mask_ref[window, :].astype(jnp.float32)
        weight_row = jnp.concatenate([weight[line : line + 1] for line in range(SIDE)], axis=1)
        decay = jnp.exp(-jnp.abs(raw))
        density = (jnp.maximum(raw, 0.0) + jnp.log1p(decay)) * weight_row
        folded = density[:, 0:columns]
        for line in range(1, SIDE):
            folded = folded + density[:, line * columns : (line + 1) * columns]
        column = lax.broadcasted_iota(jnp.int32, (columns, blocks), 0)
        block = lax.broadcasted_iota(jnp.int32, (columns, blocks), 1)
        first = block - step * across
        member = ((column >= first * SIDE) & (column < first * SIDE + SIDE)).astype(jnp.float32)
        sums = exact_dot(folded, member)
        weight_sum = exact_dot(
            jnp.broadcast_to(jnp.sum(weight, axis=0, keepdims=True), (SIDE, columns)), member
        )[0:1]
        denom = jnp.maximum(weight_sum, 1.0)
        pred = sums / denom
        pred_ref[...] += pred
        pool = lax.broadcasted_iota(jnp.int32, pred.shape, 0)
        lane = lax.broadcasted_iota(jnp.int32, pred.shape, 1)
        inside = (pool < pools) & (lane >= step * across) & (lane < step * across + across)
        residual = jnp.where(inside, pred - here, 0.0)
        square_acc[...] += residual * residual
        d_block = residual / (scale * denom)
        d_columns = exact_dot(d_block, member, NT)
        d_cells = jnp.concatenate([d_columns] * SIDE, axis=1)
        d_raw = (d_cells * weight_row * jax.nn.sigmoid(raw)).astype(jnp.bfloat16)
        d_wide = d_raw.astype(jnp.float32)
        bias_sum = d_wide[:, 0:columns]
        for line in range(1, SIDE):
            bias_sum = bias_sum + d_wide[:, line * columns : (line + 1) * columns]
        bias_acc[...] += bias_sum
        out_acc[...] += dot(d_raw, hidden_two, NT)
        d_two = (dot(out_w, d_raw) * slope_two).astype(jnp.bfloat16)
        ones = jnp.ones((ONES, cells), jnp.bfloat16)
        mix_acc[...] += dot(jnp.concatenate([hidden_one, ones], axis=0), d_two, NT)
        d_one = (dot(mix, d_two) * slope_one).astype(jnp.bfloat16)
        conv_acc[...] += dot(stacked[...], d_one, NT)
        return carry

    lax.fori_loop(0, rows // SIDE, tile, 0)
    row_buf[...] = jnp.zeros_like(row_buf)
    row_buf[0:LANES, :] = bias_acc[...]
    out_bias_row = exact_dot(jnp.ones((SIDE, columns), jnp.float32), row_buf[...], NT)[0:1]
    squares = jnp.sum(jnp.sum(square_acc[...], axis=1, keepdims=True), axis=0, keepdims=True)
    conv_all = conv_acc[...]
    mix_all = mix_acc[...]
    flat_ref[0:taps, :] = conv_all[0:taps]
    flat_ref[taps : taps + width, :] = mix_all[0:width]
    base = taps + width
    flat_ref[base : base + LANES, :] = out_acc[...]
    base += LANES
    flat_ref[base:, :] = jnp.zeros((flat_ref.shape[0] - base, width), jnp.float32)
    flat_ref[base : base + 1, :] = conv_all[taps : taps + 1]
    flat_ref[base + 1 : base + 2, :] = mix_all[width : width + 1]
    flat_ref[base + 2 : base + 3, :] = out_bias_row
    flat_ref[base + 3 : base + 4, :] = jnp.broadcast_to(squares, (1, width))


def run_network(count_all, pools, x, above, below, frac, mask, here, conv, conv_bias, mix, mix_bias, out, out_bias):
    rows, channels, columns = x.shape
    taps, width = conv.shape
    blocks = here.shape[1]
    return pl.pallas_call(
        functools.partial(network_kernel, count_all, pools),
        out_shape=(
            jax.ShapeDtypeStruct((TURNS * LINES, width), jnp.float32),
            jax.ShapeDtypeStruct((LANES, blocks), jnp.float32),
        ),
        in_specs=vmem(12),
        out_specs=tuple(vmem(2)),
        scratch_shapes=[
            pltpu.VMEM((rows + 2, 3 * channels, columns), jnp.bfloat16),
            pltpu.VMEM((taps + ONES, SIDE * columns), jnp.bfloat16),
            pltpu.VMEM((width, columns), jnp.float32),
            pltpu.VMEM((taps + ONES, width), jnp.float32),
            pltpu.VMEM((width + ONES, width), jnp.float32),
            pltpu.VMEM((LANES, width), jnp.float32),
            pltpu.VMEM((LANES, columns), jnp.float32),
            pltpu.VMEM((LANES, blocks), jnp.float32),
        ],
        name="network",
    )(x, above, below, frac, mask, here, conv, conv_bias, mix, mix_bias, out, out_bias)


def finish_kernel(
    count_all, pools, sum_ref, coarse_ref,
    pred_out, conv_out, conv_bias_out, mix_out, mix_bias_out, out_out, out_bias_out, loss_out
):
    taps = conv_out.shape[0]
    width = mix_out.shape[0]
    for turn in range(TURNS):
        lines = sum_ref[turn].reshape(LINES, width)
        first = turn * LINES
        if first < taps:
            conv_out[first : first + LINES, :] = lines
        elif first < taps + width:
            mix_out[first - taps : first - taps + LINES, :] = lines
        elif first == taps + width:
            out_out[...] = lines[0:pools]
            conv_bias_out[...] = lines[LANES : LANES + 1]
            mix_bias_out[...] = lines[LANES + 1 : LANES + 2]
            out_bias_out[...] = lines[LANES + 2 : LANES + 3, 0:pools]
            loss_out[...] = 0.5 * lines[LANES + 3 : LANES + 4, 0:1] / count_all
    pred_out[...] = coarse_ref[0:pools, :]


def finish(count_all, pools, taps, summed, coarse):
    width = summed.shape[-1]
    shapes = [
        (pools, coarse.shape[1]), (taps, width), (1, width), (width, width), (1, width), (pools, width),
        (1, pools), (1, 1),
    ]
    return pl.pallas_call(
        functools.partial(finish_kernel, count_all, pools),
        out_shape=tuple(jax.ShapeDtypeStruct(shape, jnp.float32) for shape in shapes),
        in_specs=vmem(2),
        out_specs=tuple(vmem(len(shapes))),
        name="finish",
    )(summed, coarse)


def on_device(
    fields,
    land_mask,
    land_frac,
    owner_map,
    targets,
    conv_weight,
    conv_bias,
    mix_weight,
    mix_bias,
    out_weight,
    out_bias,
):
    peers = lax.axis_size("space")
    pools = out_weight.shape[1]
    width = conv_bias.shape[0]
    blocks = fields.shape[2] // SIDE * (fields.shape[3] // SIDE)
    count_all = lax.axis_size("dp") * pools * owner_map.shape[0]
    x = fields[0].transpose(1, 0, 2)
    above, below = halo_rows(x)
    strip, owner, here = route_targets(owner_map, targets[0], peers, blocks)
    conv = conv_weight.reshape(-1, width)
    flat, pred = run_network(
        count_all, pools, x, above, below, land_frac, land_mask, here, conv, conv_bias[None],
        mix_weight, mix_bias[None], out_weight.T, out_bias[None],
    )
    summed, coarse = reduce_all(
        flat.reshape(TURNS, LINES, width), pred, strip, owner, peers, blocks
    )
    pred_out, conv_out, conv_bias_out, mix_out, mix_bias_out, out_out, out_bias_out, loss = finish(
        count_all, pools, conv.shape[0], summed, coarse
    )
    return (
        pred_out[None],
        conv_out.reshape(conv_weight.shape),
        conv_bias_out[0],
        mix_out,
        mix_bias_out[0],
        out_out.T,
        out_bias_out[0],
        loss[0, 0],
    )


def solution(mesh):
    placed = (
        P("dp", None, "space", None),
        P("space", None),
        P("space", None),
        P(),
        P("dp", None, "space"),
        P(),
        P(),
        P(),
        P(),
        P(),
        P(),
    )
    return jax.shard_map(
        on_device,
        mesh=mesh,
        in_specs=placed,
        out_specs=(P("dp", None, "space"), P(), P(), P(), P(), P(), P(), P()),
        check_vma=False,
    )
```

```python
import functools
import math

import jax
import jax.numpy as jnp
from jax import lax
from jax.experimental import pallas as pl
from jax.experimental.pallas import tpu as pltpu
from jax.sharding import PartitionSpec as P

SIDE = 8


CUBIC = 0.044715
ROOT_TWO_PI = math.sqrt(2.0 / math.pi)


def gelu_pair(pre):
    inner = ROOT_TWO_PI * (pre + CUBIC * pre * pre * pre)
    tanh_value = jnp.tanh(inner)
    value = 0.5 * pre * (1.0 + tanh_value)
    slope = 0.5 * (1.0 + tanh_value) + 0.5 * pre * (1.0 - tanh_value * tanh_value) * ROOT_TWO_PI * (
        1.0 + 3.0 * CUBIC * pre * pre
    )
    return (value, slope)


MESH = pl.DeviceIdType.MESH
EXACT = lax.Precision.HIGHEST
TURNS = 16
LINES = 32
PART = 2
SLOTS = 3
LANES = 16


def pack(values, picks):
    peers = picks[0].shape[0]
    rows = [
        lax.dot_general(values, pick, (((1,), (1,)), ((), ())), precision=EXACT, preferred_element_type=jnp.float32)
        for pick in picks
    ]
    rows.append(jnp.zeros((128 - LANES * len(picks), peers), jnp.float32))
    return jnp.concatenate(rows, axis=0).T


def unpack(block, picks):
    turned = block.T
    total = None
    for slot, pick in enumerate(picks):
        term = jnp.dot(
            turned[LANES * slot : LANES * (slot + 1)], pick, precision=EXACT, preferred_element_type=jnp.float32
        )
        total = term if total is None else total + term
    return total


def owner_picks(owners, me, blocks):
    peers = owners.shape[0]
    local = owners - me * blocks
    match = ((local >= 0) & (local < blocks)).astype(jnp.float32)
    row = lax.broadcasted_iota(jnp.int32, (blocks, blocks), 0)
    col = lax.broadcasted_iota(jnp.int32, (blocks, blocks), 1)
    before = (row < col).astype(jnp.float32)
    earlier = jnp.dot(match.astype(jnp.bfloat16), before.astype(jnp.bfloat16), preferred_element_type=jnp.float32)
    place = lax.broadcasted_iota(jnp.int32, (peers, blocks), 1).astype(jnp.float32)
    picks = []
    for slot in range(SLOTS):
        mine = match * (earlier == float(slot)).astype(jnp.float32)
        spot = jnp.sum(mine * local.astype(jnp.float32), axis=1, keepdims=True)
        picks.append((place == spot).astype(jnp.float32))
    return picks


def strip_picks(owned, peers, blocks):
    scaled = (owned.astype(jnp.float32) + 0.5) * (1.0 / blocks)
    target = jnp.floor(scaled)
    row = lax.broadcasted_iota(jnp.int32, (blocks, blocks), 0)
    col = lax.broadcasted_iota(jnp.int32, (blocks, blocks), 1)
    spread = jnp.broadcast_to(target, (blocks, blocks))
    column = jnp.sum(jnp.where(row == col, spread, 0.0), axis=1, keepdims=True)
    same = jnp.where((column == spread) & (row < col), 1.0, 0.0)
    rank = jnp.sum(same, axis=0, keepdims=True)
    peer = lax.broadcasted_iota(jnp.int32, (peers, blocks), 0).astype(jnp.float32)
    return [
        ((peer == target) & (rank == float(slot))).astype(jnp.float32) for slot in range(SLOTS)
    ]


def row_copy(peers, me, step, send_ref, recv_ref, send_sems, recv_sems):
    peer = lax.rem(me + step, peers)
    return pltpu.make_async_remote_copy(
        src_ref=send_ref.at[peer],
        dst_ref=recv_ref.at[me],
        send_sem=send_sems.at[step],
        recv_sem=recv_sems.at[step],
        device_id=(lax.axis_index("dp"), peer),
        device_id_type=MESH,
    )


def vmem(count):
    return [pl.BlockSpec(memory_space=pltpu.VMEM)] * count


NT = (((1,), (1,)), ((), ()))
ONES = 16
EARLY = 6


def dot(left, right, dims=(((1,), (0,)), ((), ()))):
    return lax.dot_general(left, right, dims, preferred_element_type=jnp.float32)


def exact_dot(left, right, dims=(((1,), (0,)), ((), ()))):
    return lax.dot_general(left, right, dims, precision=EXACT, preferred_element_type=jnp.float32)


def column_of(row):
    width = row.shape[1]
    return jnp.broadcast_to(row, (width, width)).T[:, 0:1]


def shift_rows(block):
    wide = block.astype(jnp.float32)
    columns = wide.shape[2]
    place = lax.broadcasted_iota(jnp.int32, wide.shape, 2)
    left = jnp.where(place == 0, 0.0, pltpu.roll(wide, 1, 2))
    right = jnp.where(place == columns - 1, 0.0, pltpu.roll(wide, columns - 1, 2))
    return jnp.concatenate([left.astype(jnp.bfloat16), block, right.astype(jnp.bfloat16)], axis=1)


def step_kernel(
    peers, ways, count_all, pools,
    x_ref, frac_ref, mask_ref, owners_ref, targets_ref,
    conv_ref, conv_bias_ref, mix_ref, mix_bias_ref, out_ref, out_bias_ref,
    sum_ref, coarse_ref,
    shifted, stacked, hidden_one, hidden_two, slope_one, slope_two, gain,
    row_buf, conv_acc, mix_acc, out_acc, bias_acc, sums_acc, weight_acc, flat,
    square_acc, conv_tr, mix_tr, out_tr, out_wr, picks, edge, target_send, target_recv, pred_send, pred_recv, got, part, got_part, whole,
    edge_out, edge_in, target_out, target_in, pred_out, pred_in, out_sems, in_sems, own_sem
):
    me = lax.axis_index("space")
    x = lax.axis_index("dp")
    span = ways * 2
    z = me // span
    y = lax.rem(me, span) // 2
    core = lax.rem(me, 2)
    rank = x * ways + y
    deep = z * 2 + core
    rows, channels, columns = x_ref.shape
    taps, width = conv_ref.shape
    cells = SIDE * columns
    tiles = rows // SIDE
    blocks = owners_ref.shape[1]
    across = columns // SIDE
    scale = math.sqrt(count_all)

    def plane(step):
        other = lax.rem(rank + step, TURNS)
        return other, (other // ways, z * span + lax.rem(other, ways) * 2 + core)

    def line(step):
        other = lax.rem(deep + step, TURNS)
        return other, (x, (other // 2) * span + y * 2 + lax.rem(other, 2))

    barrier = pltpu.get_barrier_semaphore()

    def greet(step, carry):
        pl.semaphore_signal(barrier, inc=1, device_id=(x, lax.rem(me + step, peers)), device_id_type=MESH)
        return carry

    def greet_plane(step, carry):
        pl.semaphore_signal(barrier, inc=1, device_id=plane(step)[1], device_id_type=MESH)
        return carry

    lax.fori_loop(1, peers, greet, 0)
    lax.fori_loop(1, TURNS, greet_plane, 0)

    owner = owner_picks(owners_ref[...], me, blocks)
    strip = strip_picks(owners_ref[pl.ds(me, 1), :], peers, blocks)
    for slot in range(SLOTS):
        picks[slot] = strip[slot]
        picks[SLOTS + slot] = owner[slot]
    sums_acc[...] = jnp.zeros_like(sums_acc)
    sums_acc[0:pools, :] = targets_ref[:, 0, :]
    target_send[:, 0, :] = pack(sums_acc[...], owner)

    def shift_some(step, carry):
        shifted[pl.ds(step * SIDE + 1, SIDE)] = shift_rows(x_ref[pl.ds(step * SIDE, SIDE)])
        return carry

    lax.fori_loop(0, tiles, shift_some, 0)

    def fill_ones(step, carry):
        stacked[step, taps : taps + ONES, :] = jnp.ones((ONES, cells), jnp.bfloat16)
        hidden_one[step, width : width + ONES, :] = jnp.ones((ONES, cells), jnp.bfloat16)
        return carry

    lax.fori_loop(0, tiles, fill_ones, 0)

    conv_t = conv_ref[...].astype(jnp.float32).T.astype(jnp.bfloat16)
    mix = mix_ref[...]
    mix_t = mix.astype(jnp.float32).T.astype(jnp.bfloat16)
    row_buf[...] = jnp.zeros_like(row_buf)
    row_buf[0:pools, :] = out_ref[...].astype(jnp.float32)
    out_wide = row_buf[...]
    out_t = out_wide[0:LANES].astype(jnp.bfloat16)
    out_w = out_wide.T[:, 0:LANES].astype(jnp.bfloat16)
    row_buf[...] = jnp.zeros_like(row_buf)
    row_buf[0:1, 0:pools] = out_bias_ref[...]
    conv_bias = column_of(conv_bias_ref[...])
    mix_bias = column_of(mix_bias_ref[...])
    out_bias = column_of(row_buf[0:1, :])[0:LANES]

    conv_tr[...] = conv_t
    mix_tr[...] = mix_t
    out_tr[...] = out_t
    out_wr[...] = out_w
    conv_acc[...] = jnp.zeros_like(conv_acc)
    mix_acc[...] = jnp.zeros_like(mix_acc)
    out_acc[...] = jnp.zeros_like(out_acc)
    bias_acc[...] = jnp.zeros_like(bias_acc)
    sums_acc[...] = jnp.zeros_like(sums_acc)
    weight_acc[...] = jnp.zeros_like(weight_acc)

    def members(step):
        column = lax.broadcasted_iota(jnp.int32, (columns, blocks), 0)
        first = (lax.broadcasted_iota(jnp.int32, (columns, blocks), 1) - step * across) * SIDE
        return ((column >= first) & (column < first + SIDE)).astype(jnp.float32)

    def forward(step, carry):
        base = step * SIDE
        for turn in range(SIDE):
            window = shifted[pl.ds(base + turn, 3)]
            stacked[step, 0:taps, turn * columns : (turn + 1) * columns] = window.reshape(taps, columns)
        pre_one = dot(conv_tr[...], stacked[step, 0:taps, :]) + conv_bias
        value_one, slope = gelu_pair(pre_one)
        slope_one[step] = slope
        narrow = value_one.astype(jnp.bfloat16)
        hidden_one[step, 0:width, :] = narrow
        pre_two = dot(mix_tr[...], narrow) + mix_bias
        value_two, slope = gelu_pair(pre_two)
        slope_two[step] = slope
        narrow = value_two.astype(jnp.bfloat16)
        hidden_two[step] = narrow
        raw = dot(out_tr[...], narrow) + out_bias
        window = pl.ds(pl.multiple_of(base, SIDE), SIDE)
        weight = frac_ref[window, :] * mask_ref[window, :].astype(jnp.float32)
        weight_row = jnp.concatenate([weight[turn : turn + 1] for turn in range(SIDE)], axis=1)
        density = (jnp.maximum(raw, 0.0) + jnp.log1p(jnp.exp(-jnp.abs(raw)))) * weight_row
        gain[step] = weight_row * jax.nn.sigmoid(raw)
        folded = density[:, 0:columns]
        for turn in range(1, SIDE):
            folded = folded + density[:, turn * columns : (turn + 1) * columns]
        member = members(step)
        sums_acc[...] += exact_dot(folded, member)
        weight_acc[...] += exact_dot(
            jnp.broadcast_to(jnp.sum(weight, axis=0, keepdims=True), (SIDE, columns)), member
        )
        return carry

    def edge_copy(side):
        peer = lax.rem(me + (1 if side == 0 else peers - 1), peers)
        return pltpu.make_async_remote_copy(
            src_ref=x_ref.at[rows - 1 if side == 0 else 0],
            dst_ref=edge.at[side],
            send_sem=edge_out.at[side],
            recv_sem=edge_in.at[side],
            device_id=(x, peer),
            device_id_type=MESH,
        )

    def routed(send, recv, outs, ins):
        def begin(step, carry):
            row_copy(peers, me, step, send, recv, outs, ins).start()
            return carry

        def finish(step, carry):
            row_copy(peers, me, step, send, recv, outs, ins).wait()
            return carry

        return (
            lambda: lax.fori_loop(1, peers, begin, 0),
            lambda: lax.fori_loop(1, peers, finish, 0),
        )

    start_targets, wait_targets = routed(target_send, target_recv, target_out, target_in)
    start_pred, wait_pred = routed(pred_send, pred_recv, pred_out, pred_in)

    lax.fori_loop(1, EARLY, forward, 0)
    pl.semaphore_wait(barrier, peers - 1 + TURNS - 1)
    for side in range(2):
        edge_copy(side).start()
    start_targets()
    target_recv[pl.ds(me, 1)] = target_send[pl.ds(me, 1)]
    lax.fori_loop(EARLY, tiles - 1, forward, 0)
    for side in range(2):
        edge_copy(side).wait()
    keep_above = jnp.where(me == 0, 0.0, 1.0)
    keep_below = jnp.where(me == peers - 1, 0.0, 1.0)
    edges = edge[...].astype(jnp.float32)
    shifted[0:1] = shift_rows((edges[0:1] * keep_above).astype(jnp.bfloat16))
    shifted[rows + 1 : rows + 2] = shift_rows((edges[1:2] * keep_below).astype(jnp.bfloat16))
    lax.fori_loop(0, 2, lambda turn, carry: forward(turn * (tiles - 1), carry), 0)

    wait_targets()

    @pl.when(me >= 0)
    def _():
        denom = jnp.maximum(weight_acc[0:1, :], 1.0)
        pred = sums_acc[...] / denom
        pred_send[:, 0, :] = pack(pred, [picks[slot] for slot in range(SLOTS)])
        here = unpack(target_recv[:, 0, :], [picks[slot] for slot in range(SLOTS)])
        pool = lax.broadcasted_iota(jnp.int32, pred.shape, 0)
        residual = jnp.where(pool < pools, pred - here, 0.0)
        square_acc[...] = jnp.broadcast_to(jnp.sum(jnp.sum(residual * residual, axis=1, keepdims=True), axis=0, keepdims=True), square_acc.shape)
        sums_acc[...] = residual / (scale * denom)

    start_pred()
    pred_recv[pl.ds(me, 1)] = pred_send[pl.ds(me, 1)]

    def backward(step, carry):
        d_columns = exact_dot(sums_acc[...], members(step), NT)
        d_raw = (jnp.concatenate([d_columns] * SIDE, axis=1) * gain[step]).astype(jnp.bfloat16)
        d_wide = d_raw.astype(jnp.float32)
        bias_sum = d_wide[:, 0:columns]
        for turn in range(1, SIDE):
            bias_sum = bias_sum + d_wide[:, turn * columns : (turn + 1) * columns]
        bias_acc[...] += bias_sum
        out_acc[...] += dot(d_raw, hidden_two[step], NT)
        d_two = (dot(out_wr[...], d_raw) * slope_two[step]).astype(jnp.bfloat16)
        mix_acc[...] += dot(hidden_one[step], d_two, NT)
        d_one = (dot(mix_ref[...], d_two) * slope_one[step]).astype(jnp.bfloat16)
        conv_acc[...] += dot(stacked[step], d_one, NT)
        return carry

    lax.fori_loop(0, tiles, backward, 0)

    row_buf[...] = jnp.zeros_like(row_buf)
    row_buf[0:LANES, :] = bias_acc[...]
    out_bias_row = exact_dot(jnp.ones((SIDE, columns), jnp.float32), row_buf[...], NT)[0:1]
    base = taps + width + LANES
    flat[base:, :] = jnp.zeros((TURNS * LINES - base, width), jnp.float32)
    flat[base : base + 1, :] = conv_acc[taps : taps + 1]
    flat[base + 1 : base + 2, :] = mix_acc[width : width + 1]
    flat[base + 2 : base + 3, :] = out_bias_row
    flat[base + 3 : base + 4, :] = square_acc[0:1]
    flat[0:taps, :] = conv_acc[0:taps]
    flat[taps : taps + width, :] = mix_acc[0:width]
    flat[taps + width : base, :] = out_acc[...]

    def lines(index):
        return pl.ds(pl.multiple_of(index * LINES, LINES), LINES)

    def remote(src, dst, phase, step, device):
        return pltpu.make_async_remote_copy(
            src_ref=src,
            dst_ref=dst,
            send_sem=out_sems.at[phase, step],
            recv_sem=in_sems.at[phase, step],
            device_id=device,
            device_id_type=MESH,
        )

    def scatter_plane(step):
        other, device = plane(step)
        return remote(flat.at[lines(other)], got.at[step - 1], 0, step, device)

    def scatter_line(step):
        other, device = line(step)
        return remote(part.at[other], got_part.at[step - 1], 1, step, device)

    def gather_line(step):
        return remote(whole.at[deep], whole.at[deep], 2, step, line(step)[1])

    def gather_plane(step):
        return remote(sum_ref.at[rank], sum_ref.at[rank], 3, step, plane(step)[1])

    def start_all(build):
        def body(step, carry):
            build(step).start()
            return carry

        lax.fori_loop(1, TURNS, body, 0)

    def wait_all(build):
        def body(step, carry):
            build(step).wait()
            return carry

        lax.fori_loop(1, TURNS, body, 0)

    start_all(scatter_plane)
    wait_pred()
    coarse_ref[...] = unpack(pred_recv[:, 0, :], [picks[SLOTS + slot] for slot in range(SLOTS)])
    wait_all(scatter_plane)
    total = flat[lines(rank), :]
    for step in range(TURNS - 1):
        total = total + got[step]
    for turn in range(TURNS):
        part[turn] = total[PART * turn : PART * (turn + 1)]
    start_all(scatter_line)
    wait_all(scatter_line)
    piece = part[deep]
    for step in range(TURNS - 1):
        piece = piece + got_part[step]
    whole[deep] = piece
    start_all(gather_line)
    wait_all(gather_line)
    own = pltpu.make_async_copy(whole, sum_ref.at[rank], own_sem)
    own.start()
    own.wait()
    start_all(gather_plane)
    wait_all(gather_plane)


def run_step(
    peers, count_all, pools, x, frac, mask, owners, targets, conv, conv_bias, mix, mix_bias, out, out_bias
):
    rows, channels, columns = x.shape
    taps, width = conv.shape
    blocks = owners.shape[1]
    tiles = rows // SIDE
    cells = SIDE * columns
    f32, bf16 = jnp.float32, jnp.bfloat16
    return pl.pallas_call(
        functools.partial(step_kernel, peers, lax.axis_size("dp"), count_all, pools),
        out_shape=(
            jax.ShapeDtypeStruct((TURNS, TURNS, PART, width), f32),
            jax.ShapeDtypeStruct((LANES, blocks), f32),
        ),
        in_specs=vmem(11),
        out_specs=tuple(vmem(2)),
        scratch_shapes=[
            pltpu.VMEM((rows + 2, 3 * channels, columns), bf16),
            pltpu.VMEM((tiles, taps + ONES, cells), bf16),
            pltpu.VMEM((tiles, width + ONES, cells), bf16),
            pltpu.VMEM((tiles, width, cells), bf16),
            pltpu.VMEM((tiles, width, cells), f32),
            pltpu.VMEM((tiles, width, cells), f32),
            pltpu.VMEM((tiles, LANES, cells), f32),
            pltpu.VMEM((width, columns), f32),
            pltpu.VMEM((taps + ONES, width), f32),
            pltpu.VMEM((width + ONES, width), f32),
            pltpu.VMEM((LANES, width), f32),
            pltpu.VMEM((LANES, columns), f32),
            pltpu.VMEM((LANES, blocks), f32),
            pltpu.VMEM((SIDE, blocks), f32),
            pltpu.VMEM((TURNS * LINES, width), f32),
            pltpu.VMEM((SIDE, width), f32),
            pltpu.VMEM((width, taps), bf16),
            pltpu.VMEM((width, width), bf16),
            pltpu.VMEM((LANES, width), bf16),
            pltpu.VMEM((width, LANES), bf16),
            pltpu.VMEM((2 * SLOTS, peers, blocks), f32),
            pltpu.VMEM((2, channels, columns), bf16),
            pltpu.VMEM((peers, 1, 128), f32),
            pltpu.VMEM((peers, 1, 128), f32),
            pltpu.VMEM((peers, 1, 128), f32),
            pltpu.VMEM((peers, 1, 128), f32),
            pltpu.VMEM((TURNS - 1, LINES, width), f32),
            pltpu.VMEM((TURNS, PART, width), f32),
            pltpu.VMEM((TURNS - 1, PART, width), f32),
            pltpu.VMEM((TURNS, PART, width), f32),
            pltpu.SemaphoreType.DMA((2,)),
            pltpu.SemaphoreType.DMA((2,)),
            pltpu.SemaphoreType.DMA((peers,)),
            pltpu.SemaphoreType.DMA((peers,)),
            pltpu.SemaphoreType.DMA((peers,)),
            pltpu.SemaphoreType.DMA((peers,)),
            pltpu.SemaphoreType.DMA((4, TURNS)),
            pltpu.SemaphoreType.DMA((4, TURNS)),
            pltpu.SemaphoreType.DMA,
        ],
        compiler_params=pltpu.CompilerParams(collective_id=0, has_side_effects=True),
        name="train_step",
    )(x, frac, mask, owners, targets, conv, conv_bias, mix, mix_bias, out, out_bias)


def finish_kernel(
    count_all, pools, sum_ref, coarse_ref,
    pred_out, conv_out, conv_bias_out, mix_out, mix_bias_out, out_out, out_bias_out, loss_out
):
    taps = conv_out.shape[0]
    width = mix_out.shape[0]
    for turn in range(TURNS):
        lines = sum_ref[turn].reshape(LINES, width)
        first = turn * LINES
        if first < taps:
            conv_out[first : first + LINES, :] = lines
        elif first < taps + width:
            mix_out[first - taps : first - taps + LINES, :] = lines
        elif first == taps + width:
            out_out[...] = lines[0:pools]
            conv_bias_out[...] = lines[LANES : LANES + 1]
            mix_bias_out[...] = lines[LANES + 1 : LANES + 2]
            out_bias_out[...] = lines[LANES + 2 : LANES + 3, 0:pools]
            loss_out[...] = 0.5 * lines[LANES + 3 : LANES + 4, 0:1] / count_all
    pred_out[:, 0, :] = coarse_ref[0:pools, :]


def finish(count_all, pools, taps, summed, coarse):
    width = summed.shape[-1]
    shapes = [
        (pools, 1, coarse.shape[1]), (taps, width), (1, width), (width, width), (1, width), (pools, width),
        (1, pools), (1, 1),
    ]
    return pl.pallas_call(
        functools.partial(finish_kernel, count_all, pools),
        out_shape=tuple(jax.ShapeDtypeStruct(shape, jnp.float32) for shape in shapes),
        in_specs=vmem(2),
        out_specs=tuple(vmem(len(shapes))),
        name="finish",
    )(summed, coarse)


def on_device(
    fields,
    land_mask,
    land_frac,
    owner_map,
    targets,
    conv_weight,
    conv_bias,
    mix_weight,
    mix_bias,
    out_weight,
    out_bias,
):
    peers = lax.axis_size("space")
    pools = out_weight.shape[1]
    width = conv_bias.shape[0]
    blocks = fields.shape[2] // SIDE * (fields.shape[3] // SIDE)
    count_all = lax.axis_size("dp") * pools * owner_map.shape[0]
    x = fields[0].transpose(1, 0, 2)
    conv = conv_weight.reshape(-1, width)
    summed, coarse = run_step(
        peers, count_all, pools, x, land_frac, land_mask, owner_map.reshape(peers, blocks),
        targets.transpose(1, 0, 2), conv, conv_bias[None], mix_weight, mix_bias[None],
        out_weight.T, out_bias[None],
    )
    pred_out, conv_out, conv_bias_out, mix_out, mix_bias_out, out_out, out_bias_out, loss = finish(
        count_all, pools, conv.shape[0], summed, coarse
    )
    return (
        pred_out.transpose(1, 0, 2),
        conv_out.reshape(conv_weight.shape),
        conv_bias_out[0],
        mix_out,
        mix_bias_out[0],
        out_out.T,
        out_bias_out[0],
        loss[0, 0],
    )


def solution(mesh):
    placed = (
        P("dp", None, "space", None),
        P("space", None),
        P("space", None),
        P(),
        P("dp", None, "space"),
        P(),
        P(),
        P(),
        P(),
        P(),
        P(),
    )
    return jax.shard_map(
        on_device,
        mesh=mesh,
        in_specs=placed,
        out_specs=(P("dp", None, "space"), P(), P(), P(), P(), P(), P(), P()),
        check_vma=False,
    )
```

```python
import functools
import math

import jax
import jax.numpy as jnp
from jax import lax
from jax.experimental import pallas as pl
from jax.experimental.pallas import tpu as pltpu
from jax.sharding import PartitionSpec as P

SIDE = 8


CUBIC = 0.044715
ROOT_TWO_PI = math.sqrt(2.0 / math.pi)


def gelu_pair(pre):
    square = pre * pre
    gate = 0.5 + 0.5 * jnp.tanh(pre * (ROOT_TWO_PI + ROOT_TWO_PI * CUBIC * square))
    rate = 2.0 * ROOT_TWO_PI + 6.0 * ROOT_TWO_PI * CUBIC * square
    return (pre * gate, gate + pre * rate * (gate - gate * gate))


MESH = pl.DeviceIdType.MESH
EXACT = lax.Precision.HIGHEST
TURNS = 16
LINES = 32
PART = 2
SLOTS = 3
LANES = 16


def pack(values, picks):
    peers = picks[0].shape[0]
    rows = [
        lax.dot_general(values, pick, (((1,), (1,)), ((), ())), precision=EXACT, preferred_element_type=jnp.float32)
        for pick in picks
    ]
    rows.append(jnp.zeros((128 - LANES * len(picks), peers), jnp.float32))
    return jnp.concatenate(rows, axis=0).T


def unpack(block, picks):
    turned = block.T
    total = None
    for slot, pick in enumerate(picks):
        term = jnp.dot(
            turned[LANES * slot : LANES * (slot + 1)], pick, precision=EXACT, preferred_element_type=jnp.float32
        )
        total = term if total is None else total + term
    return total


def owner_picks(owners, me, blocks):
    peers = owners.shape[0]
    local = owners - me * blocks
    match = ((local >= 0) & (local < blocks)).astype(jnp.float32)
    row = lax.broadcasted_iota(jnp.int32, (blocks, blocks), 0)
    col = lax.broadcasted_iota(jnp.int32, (blocks, blocks), 1)
    before = (row < col).astype(jnp.float32)
    earlier = jnp.dot(match.astype(jnp.bfloat16), before.astype(jnp.bfloat16), preferred_element_type=jnp.float32)
    place = lax.broadcasted_iota(jnp.int32, (peers, blocks), 1).astype(jnp.float32)
    picks = []
    for slot in range(SLOTS):
        mine = match * (earlier == float(slot)).astype(jnp.float32)
        spot = jnp.sum(mine * local.astype(jnp.float32), axis=1, keepdims=True)
        picks.append((place == spot).astype(jnp.float32))
    return picks


def strip_picks(owned, peers, blocks):
    scaled = (owned.astype(jnp.float32) + 0.5) * (1.0 / blocks)
    target = jnp.floor(scaled)
    row = lax.broadcasted_iota(jnp.int32, (blocks, blocks), 0)
    col = lax.broadcasted_iota(jnp.int32, (blocks, blocks), 1)
    spread = jnp.broadcast_to(target, (blocks, blocks))
    column = jnp.sum(jnp.where(row == col, spread, 0.0), axis=1, keepdims=True)
    same = jnp.where((column == spread) & (row < col), 1.0, 0.0)
    rank = jnp.sum(same, axis=0, keepdims=True)
    peer = lax.broadcasted_iota(jnp.int32, (peers, blocks), 0).astype(jnp.float32)
    return [
        ((peer == target) & (rank == float(slot))).astype(jnp.float32) for slot in range(SLOTS)
    ]


def row_copy(peers, me, step, send_ref, recv_ref, send_sems, recv_sems):
    peer = lax.rem(me + step, peers)
    return pltpu.make_async_remote_copy(
        src_ref=send_ref.at[peer],
        dst_ref=recv_ref.at[me],
        send_sem=send_sems.at[step],
        recv_sem=recv_sems.at[step],
        device_id=(lax.axis_index("dp"), peer),
        device_id_type=MESH,
    )


def vmem(count):
    return [pl.BlockSpec(memory_space=pltpu.VMEM)] * count


NT = (((1,), (1,)), ((), ()))
ONES = 16
EARLY = 6


def dot(left, right, dims=(((1,), (0,)), ((), ()))):
    return lax.dot_general(left, right, dims, preferred_element_type=jnp.float32)


def exact_dot(left, right, dims=(((1,), (0,)), ((), ()))):
    return lax.dot_general(left, right, dims, precision=EXACT, preferred_element_type=jnp.float32)


def column_of(row):
    width = row.shape[1]
    return jnp.broadcast_to(row, (width, width)).T[:, 0:1]


def bias_parts(column):
    high = column.astype(jnp.bfloat16).astype(jnp.float32)
    rest = column - high
    middle = rest.astype(jnp.bfloat16).astype(jnp.float32)
    low = rest - middle
    lane = lax.broadcasted_iota(jnp.int32, (column.shape[0], ONES), 1)
    parts = jnp.where(lane == 0, high, jnp.where(lane == 1, middle, jnp.where(lane == 2, low, 0.0)))
    return parts.astype(jnp.bfloat16)


def shift_rows(block):
    wide = block.astype(jnp.float32)
    columns = wide.shape[2]
    place = lax.broadcasted_iota(jnp.int32, wide.shape, 2)
    left = jnp.where(place == 0, 0.0, pltpu.roll(wide, 1, 2))
    right = jnp.where(place == columns - 1, 0.0, pltpu.roll(wide, columns - 1, 2))
    return jnp.concatenate([left.astype(jnp.bfloat16), block, right.astype(jnp.bfloat16)], axis=1)


def step_kernel(
    peers, ways, count_all, pools,
    x_ref, frac_ref, mask_ref, owners_ref, targets_ref,
    conv_ref, conv_bias_ref, mix_ref, mix_bias_ref, out_ref, out_bias_ref,
    sum_ref, coarse_ref,
    shifted, stacked, hidden_one, hidden_two, slope_one, slope_two, gain,
    row_buf, conv_acc, mix_acc, out_acc, bias_acc, sums_acc, weight_acc, flat,
    square_acc, conv_tr, mix_tr, out_tr, out_wr, picks, edge, target_send, target_recv, pred_send, pred_recv, got, part, got_part, whole,
    edge_out, edge_in, target_out, target_in, pred_out, pred_in, out_sems, in_sems, own_sem
):
    me = lax.axis_index("space")
    x = lax.axis_index("dp")
    span = ways * 2
    z = me // span
    y = lax.rem(me, span) // 2
    core = lax.rem(me, 2)
    rank = x * ways + y
    deep = z * 2 + core
    rows, channels, columns = x_ref.shape
    taps, width = conv_ref.shape
    cells = SIDE * columns
    tiles = rows // SIDE
    blocks = owners_ref.shape[1]
    across = columns // SIDE
    scale = math.sqrt(count_all)

    def plane(step):
        other = lax.rem(rank + step, TURNS)
        return other, (other // ways, z * span + lax.rem(other, ways) * 2 + core)

    def line(step):
        other = lax.rem(deep + step, TURNS)
        return other, (x, (other // 2) * span + y * 2 + lax.rem(other, 2))

    barrier = pltpu.get_barrier_semaphore()

    def greet(step, carry):
        pl.semaphore_signal(barrier, inc=1, device_id=(x, lax.rem(me + step, peers)), device_id_type=MESH)
        return carry

    def greet_plane(step, carry):
        pl.semaphore_signal(barrier, inc=1, device_id=plane(step)[1], device_id_type=MESH)
        return carry

    lax.fori_loop(1, peers, greet, 0)
    lax.fori_loop(1, TURNS, greet_plane, 0)

    owner = owner_picks(owners_ref[...], me, blocks)
    strip = strip_picks(owners_ref[pl.ds(me, 1), :], peers, blocks)
    for slot in range(SLOTS):
        picks[slot] = strip[slot]
        picks[SLOTS + slot] = owner[slot]
    sums_acc[...] = jnp.zeros_like(sums_acc)
    sums_acc[0:pools, :] = targets_ref[:, 0, :]
    target_send[:, 0, :] = pack(sums_acc[...], owner)

    def shift_some(step, carry):
        shifted[pl.ds(step * SIDE + 1, SIDE)] = shift_rows(x_ref[pl.ds(step * SIDE, SIDE)])
        return carry

    lax.fori_loop(0, tiles, shift_some, 0)

    def fill_ones(step, carry):
        stacked[step, taps : taps + ONES, :] = jnp.ones((ONES, cells), jnp.bfloat16)
        hidden_one[step, width : width + ONES, :] = jnp.ones((ONES, cells), jnp.bfloat16)
        return carry

    lax.fori_loop(0, tiles, fill_ones, 0)

    conv_t = conv_ref[...].astype(jnp.float32).T.astype(jnp.bfloat16)
    mix = mix_ref[...]
    mix_t = mix.astype(jnp.float32).T.astype(jnp.bfloat16)
    row_buf[...] = jnp.zeros_like(row_buf)
    row_buf[0:pools, :] = out_ref[...].astype(jnp.float32)
    out_wide = row_buf[...]
    out_t = out_wide[0:LANES].astype(jnp.bfloat16)
    out_w = out_wide.T[:, 0:LANES].astype(jnp.bfloat16)
    row_buf[...] = jnp.zeros_like(row_buf)
    row_buf[0:1, 0:pools] = out_bias_ref[...]
    conv_bias = column_of(conv_bias_ref[...])
    mix_bias = column_of(mix_bias_ref[...])
    out_bias = column_of(row_buf[0:1, :])[0:LANES]

    conv_tr[:, 0:taps] = conv_t
    conv_tr[:, taps : taps + ONES] = bias_parts(conv_bias)
    mix_tr[:, 0:width] = mix_t
    mix_tr[:, width : width + ONES] = bias_parts(mix_bias)
    out_tr[...] = out_t
    out_wr[...] = out_w
    conv_acc[...] = jnp.zeros_like(conv_acc)
    mix_acc[...] = jnp.zeros_like(mix_acc)
    out_acc[...] = jnp.zeros_like(out_acc)
    bias_acc[...] = jnp.zeros_like(bias_acc)
    sums_acc[...] = jnp.zeros_like(sums_acc)
    weight_acc[...] = jnp.zeros_like(weight_acc)

    def members(step):
        column = lax.broadcasted_iota(jnp.int32, (columns, blocks), 0)
        first = (lax.broadcasted_iota(jnp.int32, (columns, blocks), 1) - step * across) * SIDE
        return ((column >= first) & (column < first + SIDE)).astype(jnp.float32)

    def forward(step, carry):
        base = step * SIDE
        for turn in range(SIDE):
            window = shifted[pl.ds(base + turn, 3)]
            stacked[step, 0:taps, turn * columns : (turn + 1) * columns] = window.reshape(taps, columns)
        pre_one = dot(conv_tr[...], stacked[step])
        value_one, slope = gelu_pair(pre_one)
        slope_one[step] = slope
        hidden_one[step, 0:width, :] = value_one.astype(jnp.bfloat16)
        pre_two = dot(mix_tr[...], hidden_one[step])
        value_two, slope = gelu_pair(pre_two)
        slope_two[step] = slope
        narrow = value_two.astype(jnp.bfloat16)
        hidden_two[step] = narrow
        raw = dot(out_tr[...], narrow) + out_bias
        window = pl.ds(pl.multiple_of(base, SIDE), SIDE)
        weight = frac_ref[window, :] * mask_ref[window, :].astype(jnp.float32)
        weight_row = jnp.concatenate([weight[turn : turn + 1] for turn in range(SIDE)], axis=1)
        density = (jnp.maximum(raw, 0.0) + jnp.log1p(jnp.exp(-jnp.abs(raw)))) * weight_row
        gain[step] = weight_row * jax.nn.sigmoid(raw)
        folded = density[:, 0:columns]
        for turn in range(1, SIDE):
            folded = folded + density[:, turn * columns : (turn + 1) * columns]
        member = members(step)
        sums_acc[...] += exact_dot(folded, member)
        weight_acc[...] += exact_dot(
            jnp.broadcast_to(jnp.sum(weight, axis=0, keepdims=True), (SIDE, columns)), member
        )
        return carry

    def edge_copy(side):
        peer = lax.rem(me + (1 if side == 0 else peers - 1), peers)
        return pltpu.make_async_remote_copy(
            src_ref=x_ref.at[rows - 1 if side == 0 else 0],
            dst_ref=edge.at[side],
            send_sem=edge_out.at[side],
            recv_sem=edge_in.at[side],
            device_id=(x, peer),
            device_id_type=MESH,
        )

    def routed(send, recv, outs, ins):
        def begin(step, carry):
            row_copy(peers, me, step, send, recv, outs, ins).start()
            return carry

        def finish(step, carry):
            row_copy(peers, me, step, send, recv, outs, ins).wait()
            return carry

        return (
            lambda: lax.fori_loop(1, peers, begin, 0),
            lambda: lax.fori_loop(1, peers, finish, 0),
        )

    start_targets, wait_targets = routed(target_send, target_recv, target_out, target_in)
    start_pred, wait_pred = routed(pred_send, pred_recv, pred_out, pred_in)

    lax.fori_loop(1, EARLY, forward, 0)
    pl.semaphore_wait(barrier, peers - 1 + TURNS - 1)
    for side in range(2):
        edge_copy(side).start()
    start_targets()
    target_recv[pl.ds(me, 1)] = target_send[pl.ds(me, 1)]
    lax.fori_loop(EARLY, tiles - 1, forward, 0)
    for side in range(2):
        edge_copy(side).wait()
    keep_above = jnp.where(me == 0, 0.0, 1.0)
    keep_below = jnp.where(me == peers - 1, 0.0, 1.0)
    edges = edge[...].astype(jnp.float32)
    shifted[0:1] = shift_rows((edges[0:1] * keep_above).astype(jnp.bfloat16))
    shifted[rows + 1 : rows + 2] = shift_rows((edges[1:2] * keep_below).astype(jnp.bfloat16))
    lax.fori_loop(0, 2, lambda turn, carry: forward(turn * (tiles - 1), carry), 0)

    wait_targets()

    @pl.when(me >= 0)
    def _():
        denom = jnp.maximum(weight_acc[0:1, :], 1.0)
        pred = sums_acc[...] / denom
        pred_send[:, 0, :] = pack(pred, [picks[slot] for slot in range(SLOTS)])
        here = unpack(target_recv[:, 0, :], [picks[slot] for slot in range(SLOTS)])
        pool = lax.broadcasted_iota(jnp.int32, pred.shape, 0)
        residual = jnp.where(pool < pools, pred - here, 0.0)
        square_acc[...] = jnp.broadcast_to(jnp.sum(jnp.sum(residual * residual, axis=1, keepdims=True), axis=0, keepdims=True), square_acc.shape)
        sums_acc[...] = residual / (scale * denom)

    start_pred()
    pred_recv[pl.ds(me, 1)] = pred_send[pl.ds(me, 1)]

    def backward(step, carry):
        d_columns = exact_dot(sums_acc[...], members(step), NT)
        d_raw = (jnp.concatenate([d_columns] * SIDE, axis=1) * gain[step]).astype(jnp.bfloat16)
        d_wide = d_raw.astype(jnp.float32)
        bias_sum = d_wide[:, 0:columns]
        for turn in range(1, SIDE):
            bias_sum = bias_sum + d_wide[:, turn * columns : (turn + 1) * columns]
        bias_acc[...] += bias_sum
        out_acc[...] += dot(d_raw, hidden_two[step], NT)
        d_two = (dot(out_wr[...], d_raw) * slope_two[step]).astype(jnp.bfloat16)
        mix_acc[...] += dot(hidden_one[step], d_two, NT)
        d_one = (dot(mix_ref[...], d_two) * slope_one[step]).astype(jnp.bfloat16)
        conv_acc[...] += dot(stacked[step], d_one, NT)
        return carry

    lax.fori_loop(0, tiles, backward, 0)

    row_buf[...] = jnp.zeros_like(row_buf)
    row_buf[0:LANES, :] = bias_acc[...]
    out_bias_row = exact_dot(jnp.ones((SIDE, columns), jnp.float32), row_buf[...], NT)[0:1]
    base = taps + width + LANES
    flat[base:, :] = jnp.zeros((TURNS * LINES - base, width), jnp.float32)
    flat[base : base + 1, :] = conv_acc[taps : taps + 1]
    flat[base + 1 : base + 2, :] = mix_acc[width : width + 1]
    flat[base + 2 : base + 3, :] = out_bias_row
    flat[base + 3 : base + 4, :] = square_acc[0:1]
    flat[0:taps, :] = conv_acc[0:taps]
    flat[taps : taps + width, :] = mix_acc[0:width]
    flat[taps + width : base, :] = out_acc[...]

    def lines(index):
        return pl.ds(pl.multiple_of(index * LINES, LINES), LINES)

    def remote(src, dst, phase, step, device):
        return pltpu.make_async_remote_copy(
            src_ref=src,
            dst_ref=dst,
            send_sem=out_sems.at[phase, step],
            recv_sem=in_sems.at[phase, step],
            device_id=device,
            device_id_type=MESH,
        )

    def scatter_plane(step):
        other, device = plane(step)
        return remote(flat.at[lines(other)], got.at[step - 1], 0, step, device)

    def scatter_line(step):
        other, device = line(step)
        return remote(part.at[other], got_part.at[step - 1], 1, step, device)

    def gather_line(step):
        return remote(whole.at[deep], whole.at[deep], 2, step, line(step)[1])

    def gather_plane(step):
        return remote(sum_ref.at[rank], sum_ref.at[rank], 3, step, plane(step)[1])

    def start_all(build):
        def body(step, carry):
            build(step).start()
            return carry

        lax.fori_loop(1, TURNS, body, 0)

    def wait_all(build):
        def body(step, carry):
            build(step).wait()
            return carry

        lax.fori_loop(1, TURNS, body, 0)

    start_all(scatter_plane)
    wait_pred()
    coarse_ref[...] = unpack(pred_recv[:, 0, :], [picks[SLOTS + slot] for slot in range(SLOTS)])
    wait_all(scatter_plane)
    total = flat[lines(rank), :]
    for step in range(TURNS - 1):
        total = total + got[step]
    for turn in range(TURNS):
        part[turn] = total[PART * turn : PART * (turn + 1)]
    start_all(scatter_line)
    wait_all(scatter_line)
    piece = part[deep]
    for step in range(TURNS - 1):
        piece = piece + got_part[step]
    whole[deep] = piece
    start_all(gather_line)
    wait_all(gather_line)
    own = pltpu.make_async_copy(whole, sum_ref.at[rank], own_sem)
    own.start()
    own.wait()
    start_all(gather_plane)
    wait_all(gather_plane)


def run_step(
    peers, count_all, pools, x, frac, mask, owners, targets, conv, conv_bias, mix, mix_bias, out, out_bias
):
    rows, channels, columns = x.shape
    taps, width = conv.shape
    blocks = owners.shape[1]
    tiles = rows // SIDE
    cells = SIDE * columns
    f32, bf16 = jnp.float32, jnp.bfloat16
    return pl.pallas_call(
        functools.partial(step_kernel, peers, lax.axis_size("dp"), count_all, pools),
        out_shape=(
            jax.ShapeDtypeStruct((TURNS, TURNS, PART, width), f32),
            jax.ShapeDtypeStruct((LANES, blocks), f32),
        ),
        in_specs=vmem(11),
        out_specs=tuple(vmem(2)),
        scratch_shapes=[
            pltpu.VMEM((rows + 2, 3 * channels, columns), bf16),
            pltpu.VMEM((tiles, taps + ONES, cells), bf16),
            pltpu.VMEM((tiles, width + ONES, cells), bf16),
            pltpu.VMEM((tiles, width, cells), bf16),
            pltpu.VMEM((tiles, width, cells), f32),
            pltpu.VMEM((tiles, width, cells), f32),
            pltpu.VMEM((tiles, LANES, cells), f32),
            pltpu.VMEM((width, columns), f32),
            pltpu.VMEM((taps + ONES, width), f32),
            pltpu.VMEM((width + ONES, width), f32),
            pltpu.VMEM((LANES, width), f32),
            pltpu.VMEM((LANES, columns), f32),
            pltpu.VMEM((LANES, blocks), f32),
            pltpu.VMEM((SIDE, blocks), f32),
            pltpu.VMEM((TURNS * LINES, width), f32),
            pltpu.VMEM((SIDE, width), f32),
            pltpu.VMEM((width, taps + ONES), bf16),
            pltpu.VMEM((width, width + ONES), bf16),
            pltpu.VMEM((LANES, width), bf16),
            pltpu.VMEM((width, LANES), bf16),
            pltpu.VMEM((2 * SLOTS, peers, blocks), f32),
            pltpu.VMEM((2, channels, columns), bf16),
            pltpu.VMEM((peers, 1, 128), f32),
            pltpu.VMEM((peers, 1, 128), f32),
            pltpu.VMEM((peers, 1, 128), f32),
            pltpu.VMEM((peers, 1, 128), f32),
            pltpu.VMEM((TURNS - 1, LINES, width), f32),
            pltpu.VMEM((TURNS, PART, width), f32),
            pltpu.VMEM((TURNS - 1, PART, width), f32),
            pltpu.VMEM((TURNS, PART, width), f32),
            pltpu.SemaphoreType.DMA((2,)),
            pltpu.SemaphoreType.DMA((2,)),
            pltpu.SemaphoreType.DMA((peers,)),
            pltpu.SemaphoreType.DMA((peers,)),
            pltpu.SemaphoreType.DMA((peers,)),
            pltpu.SemaphoreType.DMA((peers,)),
            pltpu.SemaphoreType.DMA((4, TURNS)),
            pltpu.SemaphoreType.DMA((4, TURNS)),
            pltpu.SemaphoreType.DMA,
        ],
        compiler_params=pltpu.CompilerParams(collective_id=0, has_side_effects=True),
        name="train_step",
    )(x, frac, mask, owners, targets, conv, conv_bias, mix, mix_bias, out, out_bias)


def finish_kernel(
    count_all, pools, sum_ref, coarse_ref,
    pred_out, conv_out, conv_bias_out, mix_out, mix_bias_out, out_out, out_bias_out, loss_out
):
    taps = conv_out.shape[0]
    width = mix_out.shape[0]
    for turn in range(TURNS):
        lines = sum_ref[turn].reshape(LINES, width)
        first = turn * LINES
        if first < taps:
            conv_out[first : first + LINES, :] = lines
        elif first < taps + width:
            mix_out[first - taps : first - taps + LINES, :] = lines
        elif first == taps + width:
            out_out[...] = lines[0:pools]
            conv_bias_out[...] = lines[LANES : LANES + 1]
            mix_bias_out[...] = lines[LANES + 1 : LANES + 2]
            out_bias_out[...] = lines[LANES + 2 : LANES + 3, 0:pools]
            loss_out[...] = 0.5 * lines[LANES + 3 : LANES + 4, 0:1] / count_all
    pred_out[:, 0, :] = coarse_ref[0:pools, :]


def finish(count_all, pools, taps, summed, coarse):
    width = summed.shape[-1]
    shapes = [
        (pools, 1, coarse.shape[1]), (taps, width), (1, width), (width, width), (1, width), (pools, width),
        (1, pools), (1, 1),
    ]
    return pl.pallas_call(
        functools.partial(finish_kernel, count_all, pools),
        out_shape=tuple(jax.ShapeDtypeStruct(shape, jnp.float32) for shape in shapes),
        in_specs=vmem(2),
        out_specs=tuple(vmem(len(shapes))),
        name="finish",
    )(summed, coarse)


def on_device(
    fields,
    land_mask,
    land_frac,
    owner_map,
    targets,
    conv_weight,
    conv_bias,
    mix_weight,
    mix_bias,
    out_weight,
    out_bias,
):
    peers = lax.axis_size("space")
    pools = out_weight.shape[1]
    width = conv_bias.shape[0]
    blocks = fields.shape[2] // SIDE * (fields.shape[3] // SIDE)
    count_all = lax.axis_size("dp") * pools * owner_map.shape[0]
    x = fields[0].transpose(1, 0, 2)
    conv = conv_weight.reshape(-1, width)
    summed, coarse = run_step(
        peers, count_all, pools, x, land_frac, land_mask, owner_map.reshape(peers, blocks),
        targets.transpose(1, 0, 2), conv, conv_bias[None], mix_weight, mix_bias[None],
        out_weight.T, out_bias[None],
    )
    pred_out, conv_out, conv_bias_out, mix_out, mix_bias_out, out_out, out_bias_out, loss = finish(
        count_all, pools, conv.shape[0], summed, coarse
    )
    return (
        pred_out.transpose(1, 0, 2),
        conv_out.reshape(conv_weight.shape),
        conv_bias_out[0],
        mix_out,
        mix_bias_out[0],
        out_out.T,
        out_bias_out[0],
        loss[0, 0],
    )


def solution(mesh):
    placed = (
        P("dp", None, "space", None),
        P("space", None),
        P("space", None),
        P(),
        P("dp", None, "space"),
        P(),
        P(),
        P(),
        P(),
        P(),
        P(),
    )
    return jax.shard_map(
        on_device,
        mesh=mesh,
        in_specs=placed,
        out_specs=(P("dp", None, "space"), P(), P(), P(), P(), P(), P(), P()),
        check_vma=False,
    )
```

```python
import functools
import math

import jax
import jax.numpy as jnp
from jax import lax
from jax.experimental import pallas as pl
from jax.experimental.pallas import tpu as pltpu
from jax.sharding import PartitionSpec as P

SIDE = 8


CUBIC = 0.044715
ROOT_TWO_PI = math.sqrt(2.0 / math.pi)


def gelu_pair(pre):
    square = pre * pre
    gate = 0.5 + 0.5 * jnp.tanh(pre * (ROOT_TWO_PI + ROOT_TWO_PI * CUBIC * square))
    rate = 2.0 * ROOT_TWO_PI + 6.0 * ROOT_TWO_PI * CUBIC * square
    return (pre * gate, gate + pre * rate * (gate - gate * gate))


MESH = pl.DeviceIdType.MESH
EXACT = lax.Precision.HIGHEST
TURNS = 16
LINES = 32
PART = 2
SLOTS = 3
LANES = 16


def pack(values, picks):
    peers = picks[0].shape[0]
    rows = [
        lax.dot_general(values, pick, (((1,), (1,)), ((), ())), precision=EXACT, preferred_element_type=jnp.float32)
        for pick in picks
    ]
    rows.append(jnp.zeros((128 - LANES * len(picks), peers), jnp.float32))
    return jnp.concatenate(rows, axis=0).T


def unpack(block, picks):
    turned = block.T
    total = None
    for slot, pick in enumerate(picks):
        term = jnp.dot(
            turned[LANES * slot : LANES * (slot + 1)], pick, precision=EXACT, preferred_element_type=jnp.float32
        )
        total = term if total is None else total + term
    return total


def owner_picks(owners, me, blocks):
    peers = owners.shape[0]
    local = owners - me * blocks
    match = ((local >= 0) & (local < blocks)).astype(jnp.float32)
    row = lax.broadcasted_iota(jnp.int32, (blocks, blocks), 0)
    col = lax.broadcasted_iota(jnp.int32, (blocks, blocks), 1)
    before = (row < col).astype(jnp.float32)
    earlier = jnp.dot(match.astype(jnp.bfloat16), before.astype(jnp.bfloat16), preferred_element_type=jnp.float32)
    place = lax.broadcasted_iota(jnp.int32, (peers, blocks), 1).astype(jnp.float32)
    picks = []
    for slot in range(SLOTS):
        mine = match * (earlier == float(slot)).astype(jnp.float32)
        spot = jnp.sum(mine * local.astype(jnp.float32), axis=1, keepdims=True)
        picks.append((place == spot).astype(jnp.float32))
    return picks


def strip_picks(owned, peers, blocks):
    scaled = (owned.astype(jnp.float32) + 0.5) * (1.0 / blocks)
    target = jnp.floor(scaled)
    row = lax.broadcasted_iota(jnp.int32, (blocks, blocks), 0)
    col = lax.broadcasted_iota(jnp.int32, (blocks, blocks), 1)
    spread = jnp.broadcast_to(target, (blocks, blocks))
    column = jnp.sum(jnp.where(row == col, spread, 0.0), axis=1, keepdims=True)
    same = jnp.where((column == spread) & (row < col), 1.0, 0.0)
    rank = jnp.sum(same, axis=0, keepdims=True)
    peer = lax.broadcasted_iota(jnp.int32, (peers, blocks), 0).astype(jnp.float32)
    return [
        ((peer == target) & (rank == float(slot))).astype(jnp.float32) for slot in range(SLOTS)
    ]


def row_copy(peers, me, step, send_ref, recv_ref, send_sems, recv_sems):
    peer = lax.rem(me + step, peers)
    return pltpu.make_async_remote_copy(
        src_ref=send_ref.at[peer],
        dst_ref=recv_ref.at[me],
        send_sem=send_sems.at[step],
        recv_sem=recv_sems.at[step],
        device_id=(lax.axis_index("dp"), peer),
        device_id_type=MESH,
    )


def vmem(count):
    return [pl.BlockSpec(memory_space=pltpu.VMEM)] * count


NT = (((1,), (1,)), ((), ()))
ONES = 16
EARLY = 6


def dot(left, right, dims=(((1,), (0,)), ((), ()))):
    return lax.dot_general(left, right, dims, preferred_element_type=jnp.float32)


def exact_dot(left, right, dims=(((1,), (0,)), ((), ()))):
    return lax.dot_general(left, right, dims, precision=EXACT, preferred_element_type=jnp.float32)


def column_of(row):
    width = row.shape[1]
    return jnp.broadcast_to(row, (width, width)).T[:, 0:1]


def regroup(rows_ref, out_ref):
    half = out_ref.shape[0] // 2
    first, middle, last = (rows_ref[pl.ds(start, half, 3), :] for start in range(3))
    middle_turned = pltpu.roll(middle, 64, 1)
    last_turned = pltpu.roll(last, 64, 1)
    lane = lax.broadcasted_iota(jnp.int32, first.shape, 1)
    mixed = jnp.where(lane < 64, middle_turned, last_turned)
    for turn in range(half):
        out_ref[2 * turn : 2 * turn + 1, 0:128] = first[turn : turn + 1]
        out_ref[2 * turn : 2 * turn + 1, 128:192] = middle[turn : turn + 1, 0:64]
        out_ref[2 * turn + 1 : 2 * turn + 2, 0:128] = mixed[turn : turn + 1]
        out_ref[2 * turn + 1 : 2 * turn + 2, 128:192] = last_turned[turn : turn + 1, 0:64]


def bias_parts(column):
    high = column.astype(jnp.bfloat16).astype(jnp.float32)
    rest = column - high
    middle = rest.astype(jnp.bfloat16).astype(jnp.float32)
    low = rest - middle
    lane = lax.broadcasted_iota(jnp.int32, (column.shape[0], ONES), 1)
    parts = jnp.where(lane == 0, high, jnp.where(lane == 1, middle, jnp.where(lane == 2, low, 0.0)))
    return parts.astype(jnp.bfloat16)


def shift_rows(block):
    wide = block.astype(jnp.float32)
    columns = wide.shape[2]
    place = lax.broadcasted_iota(jnp.int32, wide.shape, 2)
    left = jnp.where(place == 0, 0.0, pltpu.roll(wide, 1, 2))
    right = jnp.where(place == columns - 1, 0.0, pltpu.roll(wide, columns - 1, 2))
    return jnp.concatenate([left.astype(jnp.bfloat16), block, right.astype(jnp.bfloat16)], axis=1)


def step_kernel(
    peers, ways, count_all, pools,
    x_ref, frac_ref, mask_ref, owner_rows_ref, targets_ref,
    conv_ref, conv_bias_ref, mix_ref, mix_bias_ref, out_ref, out_bias_ref,
    sum_ref, coarse_ref,
    shifted, stacked, hidden_one, hidden_two, slope_one, slope_two, gain,
    row_buf, conv_acc, mix_acc, out_acc, bias_acc, sums_acc, weight_acc, flat,
    owners_ref, square_acc, conv_tr, mix_tr, out_tr, out_wr, picks, edge, target_send, target_recv, pred_send, pred_recv, got, part, got_part, whole,
    edge_out, edge_in, target_out, target_in, pred_out, pred_in, out_sems, in_sems, own_sem
):
    me = lax.axis_index("space")
    x = lax.axis_index("dp")
    span = ways * 2
    z = me // span
    y = lax.rem(me, span) // 2
    core = lax.rem(me, 2)
    rank = x * ways + y
    deep = z * 2 + core
    rows, channels, columns = x_ref.shape
    taps, width = conv_ref.shape
    cells = SIDE * columns
    tiles = rows // SIDE
    blocks = owners_ref.shape[1]
    across = columns // SIDE
    scale = math.sqrt(count_all)

    def plane(step):
        other = lax.rem(rank + step, TURNS)
        return other, (other // ways, z * span + lax.rem(other, ways) * 2 + core)

    def line(step):
        other = lax.rem(deep + step, TURNS)
        return other, (x, (other // 2) * span + y * 2 + lax.rem(other, 2))

    barrier = pltpu.get_barrier_semaphore()

    def greet(step, carry):
        pl.semaphore_signal(barrier, inc=1, device_id=(x, lax.rem(me + step, peers)), device_id_type=MESH)
        return carry

    def greet_plane(step, carry):
        pl.semaphore_signal(barrier, inc=1, device_id=plane(step)[1], device_id_type=MESH)
        return carry

    lax.fori_loop(1, peers, greet, 0)
    lax.fori_loop(1, TURNS, greet_plane, 0)

    regroup(owner_rows_ref, owners_ref)
    owner = owner_picks(owners_ref[...], me, blocks)
    strip = strip_picks(owners_ref[pl.ds(me, 1), :], peers, blocks)
    for slot in range(SLOTS):
        picks[slot] = strip[slot]
        picks[SLOTS + slot] = owner[slot]
    sums_acc[...] = jnp.zeros_like(sums_acc)
    sums_acc[0:pools, :] = targets_ref[:, 0, :]
    target_send[:, 0, :] = pack(sums_acc[...], owner)

    def shift_some(step, carry):
        shifted[pl.ds(step * SIDE + 1, SIDE)] = shift_rows(x_ref[pl.ds(step * SIDE, SIDE)])
        return carry

    lax.fori_loop(0, tiles, shift_some, 0)

    def fill_ones(step, carry):
        stacked[step, taps : taps + ONES, :] = jnp.ones((ONES, cells), jnp.bfloat16)
        hidden_one[step, width : width + ONES, :] = jnp.ones((ONES, cells), jnp.bfloat16)
        return carry

    lax.fori_loop(0, tiles, fill_ones, 0)

    conv_t = conv_ref[...].astype(jnp.float32).T.astype(jnp.bfloat16)
    mix = mix_ref[...]
    mix_t = mix.astype(jnp.float32).T.astype(jnp.bfloat16)
    row_buf[...] = jnp.zeros_like(row_buf)
    row_buf[0:pools, :] = out_ref[...].astype(jnp.float32)
    out_wide = row_buf[...]
    out_t = out_wide[0:LANES].astype(jnp.bfloat16)
    out_w = out_wide.T[:, 0:LANES].astype(jnp.bfloat16)
    row_buf[...] = jnp.zeros_like(row_buf)
    row_buf[0:1, 0:pools] = out_bias_ref[...]
    conv_bias = column_of(conv_bias_ref[...])
    mix_bias = column_of(mix_bias_ref[...])
    out_bias = column_of(row_buf[0:1, :])[0:LANES]

    conv_tr[:, 0:taps] = conv_t
    conv_tr[:, taps : taps + ONES] = bias_parts(conv_bias)
    mix_tr[:, 0:width] = mix_t
    mix_tr[:, width : width + ONES] = bias_parts(mix_bias)
    out_tr[...] = out_t
    out_wr[...] = out_w
    conv_acc[...] = jnp.zeros_like(conv_acc)
    mix_acc[...] = jnp.zeros_like(mix_acc)
    out_acc[...] = jnp.zeros_like(out_acc)
    bias_acc[...] = jnp.zeros_like(bias_acc)
    sums_acc[...] = jnp.zeros_like(sums_acc)
    weight_acc[...] = jnp.zeros_like(weight_acc)

    def members(step):
        column = lax.broadcasted_iota(jnp.int32, (columns, blocks), 0)
        first = (lax.broadcasted_iota(jnp.int32, (columns, blocks), 1) - step * across) * SIDE
        return ((column >= first) & (column < first + SIDE)).astype(jnp.float32)

    def forward(step, carry):
        base = step * SIDE
        for turn in range(SIDE):
            window = shifted[pl.ds(base + turn, 3)]
            stacked[step, 0:taps, turn * columns : (turn + 1) * columns] = window.reshape(taps, columns)
        pre_one = dot(conv_tr[...], stacked[step])
        value_one, slope = gelu_pair(pre_one)
        slope_one[step] = slope
        hidden_one[step, 0:width, :] = value_one.astype(jnp.bfloat16)
        pre_two = dot(mix_tr[...], hidden_one[step])
        value_two, slope = gelu_pair(pre_two)
        slope_two[step] = slope
        narrow = value_two.astype(jnp.bfloat16)
        hidden_two[step] = narrow
        raw = dot(out_tr[...], narrow) + out_bias
        window = pl.ds(pl.multiple_of(base, SIDE), SIDE)
        weight = frac_ref[window, :] * mask_ref[window, :].astype(jnp.float32)
        weight_row = jnp.concatenate([weight[turn : turn + 1] for turn in range(SIDE)], axis=1)
        density = (jnp.maximum(raw, 0.0) + jnp.log1p(jnp.exp(-jnp.abs(raw)))) * weight_row
        gain[step] = weight_row * jax.nn.sigmoid(raw)
        folded = density[:, 0:columns]
        for turn in range(1, SIDE):
            folded = folded + density[:, turn * columns : (turn + 1) * columns]
        member = members(step)
        sums_acc[...] += exact_dot(folded, member)
        weight_acc[...] += exact_dot(
            jnp.broadcast_to(jnp.sum(weight, axis=0, keepdims=True), (SIDE, columns)), member
        )
        return carry

    def edge_copy(side):
        peer = lax.rem(me + (1 if side == 0 else peers - 1), peers)
        return pltpu.make_async_remote_copy(
            src_ref=x_ref.at[rows - 1 if side == 0 else 0],
            dst_ref=edge.at[side],
            send_sem=edge_out.at[side],
            recv_sem=edge_in.at[side],
            device_id=(x, peer),
            device_id_type=MESH,
        )

    def routed(send, recv, outs, ins):
        def begin(step, carry):
            row_copy(peers, me, step, send, recv, outs, ins).start()
            return carry

        def finish(step, carry):
            row_copy(peers, me, step, send, recv, outs, ins).wait()
            return carry

        return (
            lambda: lax.fori_loop(1, peers, begin, 0),
            lambda: lax.fori_loop(1, peers, finish, 0),
        )

    start_targets, wait_targets = routed(target_send, target_recv, target_out, target_in)
    start_pred, wait_pred = routed(pred_send, pred_recv, pred_out, pred_in)

    lax.fori_loop(1, EARLY, forward, 0)
    pl.semaphore_wait(barrier, peers - 1 + TURNS - 1)
    for side in range(2):
        edge_copy(side).start()
    start_targets()
    target_recv[pl.ds(me, 1)] = target_send[pl.ds(me, 1)]
    lax.fori_loop(EARLY, tiles - 1, forward, 0)
    for side in range(2):
        edge_copy(side).wait()
    keep_above = jnp.where(me == 0, 0.0, 1.0)
    keep_below = jnp.where(me == peers - 1, 0.0, 1.0)
    edges = edge[...].astype(jnp.float32)
    shifted[0:1] = shift_rows((edges[0:1] * keep_above).astype(jnp.bfloat16))
    shifted[rows + 1 : rows + 2] = shift_rows((edges[1:2] * keep_below).astype(jnp.bfloat16))
    lax.fori_loop(0, 2, lambda turn, carry: forward(turn * (tiles - 1), carry), 0)

    wait_targets()

    @pl.when(me >= 0)
    def _():
        denom = jnp.maximum(weight_acc[0:1, :], 1.0)
        pred = sums_acc[...] / denom
        pred_send[:, 0, :] = pack(pred, [picks[slot] for slot in range(SLOTS)])
        here = unpack(target_recv[:, 0, :], [picks[slot] for slot in range(SLOTS)])
        pool = lax.broadcasted_iota(jnp.int32, pred.shape, 0)
        residual = jnp.where(pool < pools, pred - here, 0.0)
        square_acc[...] = jnp.broadcast_to(jnp.sum(jnp.sum(residual * residual, axis=1, keepdims=True), axis=0, keepdims=True), square_acc.shape)
        sums_acc[...] = residual / (scale * denom)

    start_pred()
    pred_recv[pl.ds(me, 1)] = pred_send[pl.ds(me, 1)]

    def backward(step, carry):
        d_columns = exact_dot(sums_acc[...], members(step), NT)
        d_raw = (jnp.concatenate([d_columns] * SIDE, axis=1) * gain[step]).astype(jnp.bfloat16)
        d_wide = d_raw.astype(jnp.float32)
        bias_sum = d_wide[:, 0:columns]
        for turn in range(1, SIDE):
            bias_sum = bias_sum + d_wide[:, turn * columns : (turn + 1) * columns]
        bias_acc[...] += bias_sum
        out_acc[...] += dot(d_raw, hidden_two[step], NT)
        d_two = (dot(out_wr[...], d_raw) * slope_two[step]).astype(jnp.bfloat16)
        mix_acc[...] += dot(hidden_one[step], d_two, NT)
        d_one = (dot(mix_ref[...], d_two) * slope_one[step]).astype(jnp.bfloat16)
        conv_acc[...] += dot(stacked[step], d_one, NT)
        return carry

    lax.fori_loop(0, tiles, backward, 0)

    row_buf[...] = jnp.zeros_like(row_buf)
    row_buf[0:LANES, :] = bias_acc[...]
    out_bias_row = exact_dot(jnp.ones((SIDE, columns), jnp.float32), row_buf[...], NT)[0:1]
    base = taps + width + LANES
    flat[base:, :] = jnp.zeros((TURNS * LINES - base, width), jnp.float32)
    flat[base : base + 1, :] = conv_acc[taps : taps + 1]
    flat[base + 1 : base + 2, :] = mix_acc[width : width + 1]
    flat[base + 2 : base + 3, :] = out_bias_row
    flat[base + 3 : base + 4, :] = square_acc[0:1]
    flat[0:taps, :] = conv_acc[0:taps]
    flat[taps : taps + width, :] = mix_acc[0:width]
    flat[taps + width : base, :] = out_acc[...]

    def lines(index):
        return pl.ds(pl.multiple_of(index * LINES, LINES), LINES)

    def remote(src, dst, phase, step, device):
        return pltpu.make_async_remote_copy(
            src_ref=src,
            dst_ref=dst,
            send_sem=out_sems.at[phase, step],
            recv_sem=in_sems.at[phase, step],
            device_id=device,
            device_id_type=MESH,
        )

    def scatter_plane(step):
        other, device = plane(step)
        return remote(flat.at[lines(other)], got.at[step - 1], 0, step, device)

    def scatter_line(step):
        other, device = line(step)
        return remote(part.at[other], got_part.at[step - 1], 1, step, device)

    def gather_line(step):
        return remote(whole.at[deep], whole.at[deep], 2, step, line(step)[1])

    def gather_plane(step):
        return remote(sum_ref.at[rank], sum_ref.at[rank], 3, step, plane(step)[1])

    def start_all(build):
        def body(step, carry):
            build(step).start()
            return carry

        lax.fori_loop(1, TURNS, body, 0)

    def wait_all(build):
        def body(step, carry):
            build(step).wait()
            return carry

        lax.fori_loop(1, TURNS, body, 0)

    start_all(scatter_plane)
    wait_pred()
    coarse_ref[...] = unpack(pred_recv[:, 0, :], [picks[SLOTS + slot] for slot in range(SLOTS)])
    wait_all(scatter_plane)
    total = flat[lines(rank), :]
    for step in range(TURNS - 1):
        total = total + got[step]
    for turn in range(TURNS):
        part[turn] = total[PART * turn : PART * (turn + 1)]
    start_all(scatter_line)
    wait_all(scatter_line)
    piece = part[deep]
    for step in range(TURNS - 1):
        piece = piece + got_part[step]
    whole[deep] = piece
    start_all(gather_line)
    wait_all(gather_line)
    own = pltpu.make_async_copy(whole, sum_ref.at[rank], own_sem)
    own.start()
    own.wait()
    start_all(gather_plane)
    wait_all(gather_plane)


def run_step(
    peers, count_all, pools, x, frac, mask, owners, targets, conv, conv_bias, mix, mix_bias, out, out_bias
):
    rows, channels, columns = x.shape
    taps, width = conv.shape
    blocks = owners.size // peers
    tiles = rows // SIDE
    cells = SIDE * columns
    f32, bf16 = jnp.float32, jnp.bfloat16
    return pl.pallas_call(
        functools.partial(step_kernel, peers, lax.axis_size("dp"), count_all, pools),
        out_shape=(
            jax.ShapeDtypeStruct((TURNS, TURNS, PART, width), f32),
            jax.ShapeDtypeStruct((LANES, blocks), f32),
        ),
        in_specs=vmem(11),
        out_specs=tuple(vmem(2)),
        scratch_shapes=[
            pltpu.VMEM((rows + 2, 3 * channels, columns), bf16),
            pltpu.VMEM((tiles, taps + ONES, cells), bf16),
            pltpu.VMEM((tiles, width + ONES, cells), bf16),
            pltpu.VMEM((tiles, width, cells), bf16),
            pltpu.VMEM((tiles, width, cells), f32),
            pltpu.VMEM((tiles, width, cells), f32),
            pltpu.VMEM((tiles, LANES, cells), f32),
            pltpu.VMEM((width, columns), f32),
            pltpu.VMEM((taps + ONES, width), f32),
            pltpu.VMEM((width + ONES, width), f32),
            pltpu.VMEM((LANES, width), f32),
            pltpu.VMEM((LANES, columns), f32),
            pltpu.VMEM((LANES, blocks), f32),
            pltpu.VMEM((SIDE, blocks), f32),
            pltpu.VMEM((TURNS * LINES, width), f32),
            pltpu.VMEM((peers, blocks), jnp.int32),
            pltpu.VMEM((SIDE, width), f32),
            pltpu.VMEM((width, taps + ONES), bf16),
            pltpu.VMEM((width, width + ONES), bf16),
            pltpu.VMEM((LANES, width), bf16),
            pltpu.VMEM((width, LANES), bf16),
            pltpu.VMEM((2 * SLOTS, peers, blocks), f32),
            pltpu.VMEM((2, channels, columns), bf16),
            pltpu.VMEM((peers, 1, 128), f32),
            pltpu.VMEM((peers, 1, 128), f32),
            pltpu.VMEM((peers, 1, 128), f32),
            pltpu.VMEM((peers, 1, 128), f32),
            pltpu.VMEM((TURNS - 1, LINES, width), f32),
            pltpu.VMEM((TURNS, PART, width), f32),
            pltpu.VMEM((TURNS - 1, PART, width), f32),
            pltpu.VMEM((TURNS, PART, width), f32),
            pltpu.SemaphoreType.DMA((2,)),
            pltpu.SemaphoreType.DMA((2,)),
            pltpu.SemaphoreType.DMA((peers,)),
            pltpu.SemaphoreType.DMA((peers,)),
            pltpu.SemaphoreType.DMA((peers,)),
            pltpu.SemaphoreType.DMA((peers,)),
            pltpu.SemaphoreType.DMA((4, TURNS)),
            pltpu.SemaphoreType.DMA((4, TURNS)),
            pltpu.SemaphoreType.DMA,
        ],
        compiler_params=pltpu.CompilerParams(collective_id=0, has_side_effects=True),
        name="train_step",
    )(x, frac, mask, owners, targets, conv, conv_bias, mix, mix_bias, out, out_bias)


def finish_kernel(
    count_all, pools, sum_ref, coarse_ref,
    pred_out, conv_out, conv_bias_out, mix_out, mix_bias_out, out_out, out_bias_out, loss_out
):
    taps = conv_out.shape[0]
    width = mix_out.shape[0]
    for turn in range(TURNS):
        lines = sum_ref[turn].reshape(LINES, width)
        first = turn * LINES
        if first < taps:
            conv_out[first : first + LINES, :] = lines
        elif first < taps + width:
            mix_out[first - taps : first - taps + LINES, :] = lines
        elif first == taps + width:
            out_out[...] = lines[0:pools]
            conv_bias_out[...] = lines[LANES : LANES + 1]
            mix_bias_out[...] = lines[LANES + 1 : LANES + 2]
            out_bias_out[...] = lines[LANES + 2 : LANES + 3, 0:pools]
            loss_out[...] = 0.5 * lines[LANES + 3 : LANES + 4, 0:1] / count_all
    pred_out[:, 0, :] = coarse_ref[0:pools, :]


def finish(count_all, pools, taps, summed, coarse):
    width = summed.shape[-1]
    shapes = [
        (pools, 1, coarse.shape[1]), (taps, width), (1, width), (width, width), (1, width), (pools, width),
        (1, pools), (1, 1),
    ]
    return pl.pallas_call(
        functools.partial(finish_kernel, count_all, pools),
        out_shape=tuple(jax.ShapeDtypeStruct(shape, jnp.float32) for shape in shapes),
        in_specs=vmem(2),
        out_specs=tuple(vmem(len(shapes))),
        name="finish",
    )(summed, coarse)


def on_device(
    fields,
    land_mask,
    land_frac,
    owner_map,
    targets,
    conv_weight,
    conv_bias,
    mix_weight,
    mix_bias,
    out_weight,
    out_bias,
):
    peers = lax.axis_size("space")
    pools = out_weight.shape[1]
    width = conv_bias.shape[0]
    blocks = fields.shape[2] // SIDE * (fields.shape[3] // SIDE)
    count_all = lax.axis_size("dp") * pools * owner_map.shape[0]
    x = fields[0].transpose(1, 0, 2)
    conv = conv_weight.reshape(-1, width)
    summed, coarse = run_step(
        peers, count_all, pools, x, land_frac, land_mask, owner_map.reshape(-1, 128),
        targets.transpose(1, 0, 2), conv, conv_bias[None], mix_weight, mix_bias[None],
        out_weight.T, out_bias[None],
    )
    pred_out, conv_out, conv_bias_out, mix_out, mix_bias_out, out_out, out_bias_out, loss = finish(
        count_all, pools, conv.shape[0], summed, coarse
    )
    return (
        pred_out.transpose(1, 0, 2),
        conv_out.reshape(conv_weight.shape),
        conv_bias_out[0],
        mix_out,
        mix_bias_out[0],
        out_out.T,
        out_bias_out[0],
        loss[0, 0],
    )


def solution(mesh):
    placed = (
        P("dp", None, "space", None),
        P("space", None),
        P("space", None),
        P(),
        P("dp", None, "space"),
        P(),
        P(),
        P(),
        P(),
        P(),
        P(),
    )
    return jax.shard_map(
        on_device,
        mesh=mesh,
        in_specs=placed,
        out_specs=(P("dp", None, "space"), P(), P(), P(), P(), P(), P(), P()),
        check_vma=False,
    )
```
